32 devices in a mesh: dp: 4 (over x, core), fsdp: 8 (over z, y).
Axes of the slice: x: 2, y: 2, z: 4, core: 2. Of those that a mesh axis runs over, the one named last changes fastest.
Arguments:
- tokens: bfloat16 [32768, 768], P(('dp', 'fsdp')), may hold values from -6 to 6
- segment_ids: int32 [64, 512], P(('dp', 'fsdp')), may hold values from 0 to 7, never falling along the last dimension, each value on 1 to 160 neighbouring positions
- query_weight: bfloat16 [768, 768], P('fsdp'), may hold values from -0.21875 to 0.21875
- query_bias: bfloat16 [768], P('fsdp'), may hold values from -3 to 3
- key_weight: bfloat16 [768, 768], P('fsdp'), may hold values from -0.21875 to 0.21875
- value_weight: bfloat16 [768, 768], P('fsdp'), may hold values from -0.21875 to 0.21875
- value_bias: bfloat16 [768], P('fsdp'), may hold values from -3 to 3
- out_weight: bfloat16 [768, 768], P('fsdp'), may hold values from -0.625 to 0.625
- out_bias: bfloat16 [768], P('fsdp'), may hold values from -3 to 3
- first_gain: bfloat16 [768], P('fsdp'), may hold values from 0.25 to 1.75
- first_shift: bfloat16 [768], P('fsdp'), may hold values from -3 to 3
- expand_weight: bfloat16 [768, 3072], P('fsdp'), may hold values from -0.21875 to 0.21875
- expand_bias: bfloat16 [3072], P('fsdp'), may hold values from -3 to 3
- reduce_weight: bfloat16 [3072, 768], P('fsdp'), may hold values from -0.109375 to 0.109375
- reduce_bias: bfloat16 [768], P('fsdp'), may hold values from -3 to 3
- second_gain: bfloat16 [768], P('fsdp'), may hold values from 0.25 to 1.75
- second_shift: bfloat16 [768], P('fsdp'), may hold values from -3 to 3
- cotangent: bfloat16 [32768, 768], P(('dp', 'fsdp')), may hold values from -6 to 6
Outputs:
- output: bfloat16 [32768, 768], P(('dp', 'fsdp'))
- input_grad: float32 [32768, 768], P(('dp', 'fsdp'))
- grad_query_weight: float32 [768, 768], P('fsdp')
- grad_query_bias: float32 [768], P('fsdp')
- grad_key_weight: float32 [768, 768], P('fsdp')
- grad_value_weight: float32 [768, 768], P('fsdp')
- grad_value_bias: float32 [768], P('fsdp')
- grad_out_weight: float32 [768, 768], P('fsdp')
- grad_out_bias: float32 [768], P('fsdp')
- grad_first_gain: float32 [768], P('fsdp')
- grad_first_shift: float32 [768], P('fsdp')
- grad_expand_weight: float32 [768, 3072], P('fsdp')
- grad_expand_bias: float32 [3072], P('fsdp')
- grad_reduce_weight: float32 [3072, 768], P('fsdp')
- grad_reduce_bias: float32 [768], P('fsdp')
- grad_second_gain: float32 [768], P('fsdp')
- grad_second_shift: float32 [768], P('fsdp')
The draws below stay inside these ranges and needn't reach their ends.
Inputs may be any that keep to these rules, and one draw needn't show every extreme that they name: `segment_ids`: within a sequence the fragment numbers never fall; every one of the 8 fragments is present, and the longest has exactly 160 tokens.
All inputs are finite; a program needn't handle non-finite values.
Results may differ from the reference program's by a relative error of at most 0.02.
Values may be sent and summed in bfloat16 or wider, within the bound.
A program may use at most 192 MiB of HBM per device.

```python
import math
import jax
import jax.numpy as jnp
import numpy as np
from jax import lax

D = 768
HEADS = 12
HEAD = 64
FF = 3072
SEQ_LEN = 512
FRAGS = 8
MOST_FRAG = 160
SEQS = 64
TOKENS = 32768


def level_of(rng, dims, shards, low, largest):
    def one(position, shards_of):
        heights = jax.random.uniform(jax.random.fold_in(jax.random.fold_in(rng, 6), position), (shards_of,), jnp.float32, low / len(shards), largest / len(shards))
        return jnp.repeat(jnp.exp(heights), dims[position] // shards_of).reshape((-1,) + (1,) * (len(dims) - position - 1))

    factor_of = one(*shards[0])
    for cut in shards[1:]:
        factor_of = factor_of * one(*cut)
    return factor_of


def profile(count, total, reach, slope):
    loads = [(1 << 20) // math.isqrt(grade ** slope) + 1 for grade in range(2, count + 1)]
    surplus, counts = total - reach - (count - 1), [1] * (count - 1)
    while surplus > 0:
        candidates = [i for i in range(count - 1) if counts[i] < reach]
        mass, budget = sum([loads[i] for i in candidates]), surplus
        for i in candidates:
            more = min(reach - counts[i], max(1, budget * loads[i] // mass), surplus)
            counts[i] = counts[i] + more
            surplus = surplus - more
    return np.array([reach] + counts)


def ragged_sizes(rng, count, total, bound, lean):
    if count == 2:
        one = jax.random.randint(rng, (), max(1, total - bound), min(bound, total - 1) + 1)
        return jnp.stack([one, total - one])
    lengths = jnp.asarray(profile(count, total, bound, lean), jnp.int32)
    couples = (count - 1) // 2
    source_of, sink = lengths[1:1 + 2 * couples:2], lengths[2:2 + 2 * couples:2]
    slack = jnp.minimum(source_of - 1, bound - sink)
    passed = jax.random.randint(jax.random.fold_in(rng, 1), (couples,), 0, 1 << 20) % (slack + 1)
    lengths = lengths.at[1:1 + 2 * couples:2].set(source_of - passed).at[2:2 + 2 * couples:2].set(sink + passed)
    return lengths[jax.random.permutation(jax.random.fold_in(rng, 2), count)]


def scatter_about(rng, dims, deviation, reach, pieces=(), dtype=jnp.bfloat16):
    level = level_of(rng, dims, pieces, -0.22, 0.18) if pieces else 1.0
    values = jax.random.normal(rng, dims, jnp.float32) * deviation * level
    return jnp.minimum(jnp.maximum(values, -reach), reach).astype(dtype)


def setup_inputs(seed: int = 0) -> dict:
    arg_keys = jax.random.split(jax.random.key(seed), 19)
    return {
        "tokens": scatter_about(arg_keys[0], (TOKENS, D), 1.0, 6.0, ((0, 32),)),
        "segment_ids": jax.vmap(lambda own: jnp.searchsorted(jnp.cumsum(ragged_sizes(own, FRAGS, SEQ_LEN, MOST_FRAG, 1)), jnp.arange(SEQ_LEN), side="right"))(jax.random.split(arg_keys[1], SEQS)).reshape((SEQS, SEQ_LEN)).astype(jnp.int32),
        "query_weight": scatter_about(arg_keys[2], (D, D), D ** -0.5, 0.21875, ((0, 8),)),
        "query_bias": scatter_about(arg_keys[3], (D,), 0.5, 3.0, ((0, 8),)),
        "key_weight": scatter_about(arg_keys[4], (D, D), D ** -0.5, 0.21875, ((0, 8),)),
        "value_weight": scatter_about(arg_keys[5], (D, D), D ** -0.5, 0.21875, ((0, 8),)),
        "value_bias": scatter_about(arg_keys[6], (D,), 0.5, 3.0, ((0, 8),)),
        "out_weight": scatter_about(arg_keys[7], (D, D), (D // 8) ** -0.5, 0.625, ((0, 8),)),
        "out_bias": scatter_about(arg_keys[8], (D,), 0.5, 3.0, ((0, 8),)),
        "first_gain": jnp.clip(1.0 + 0.15 * jax.random.normal(arg_keys[9], (D,), jnp.float32), 0.25, 1.75).astype(jnp.bfloat16),
        "first_shift": scatter_about(arg_keys[10], (D,), 0.5, 3.0, ((0, 8),)),
        "expand_weight": scatter_about(arg_keys[11], (D, FF), D ** -0.5, 0.21875, ((0, 8),)),
        "expand_bias": scatter_about(arg_keys[12], (FF,), 0.5, 3.0, ((0, 8),)),
        "reduce_weight": scatter_about(arg_keys[13], (FF, D), FF ** -0.5, 0.109375, ((0, 8),)),
        "reduce_bias": scatter_about(arg_keys[14], (D,), 0.5, 3.0, ((0, 8),)),
        "second_gain": jnp.clip(1.0 + 0.15 * jax.random.normal(arg_keys[15], (D,), jnp.float32), 0.25, 1.75).astype(jnp.bfloat16),
        "second_shift": scatter_about(arg_keys[16], (D,), 0.5, 3.0, ((0, 8),)),
        "cotangent": scatter_about(arg_keys[17], (TOKENS, D), 1.0, 6.0, ((0, 32),)),
    }


EXACT = lax.Precision.HIGHEST

@jax.custom_vjp
def low(v):
    return lax.optimization_barrier(v.astype(jnp.bfloat16)).astype(jnp.float32)

@jax.custom_vjp
def low_back(v):
    return v

def low_keep(v):
    return (low(v), None)

def low_pass(kept, grad):
    return (grad,)

def back_keep(v):
    return (v, None)

def back_low(kept, grad):
    return (low(grad),)
low.defvjp(low_keep, low_pass)
low_back.defvjp(back_keep, back_low)

def rounded(values):
    return low(low_back(values))

def product(left, right):
    return jnp.dot(left, right, precision=EXACT, preferred_element_type=jnp.float32)

def layer_norm(rows, gain, shift):
    average = lax.optimization_barrier(jnp.mean(rows, axis=-1, keepdims=True))
    centered = rows - average
    variance = lax.optimization_barrier(jnp.mean(centered * centered, axis=-1, keepdims=True))
    return centered * lax.rsqrt(variance + 1e-12) * gain + shift

def attend(queries, key_rows, value_rows, fragment):
    scaling = HEAD ** (-0.5)
    scores = jnp.einsum('qhd,khd->hqk', queries, key_rows, precision=EXACT, preferred_element_type=jnp.float32) * scaling
    same_fragment = fragment[:, None] == fragment[None, :]
    scores = low_back(jnp.where(same_fragment[None, :, :], scores, -1000000000.0))
    weights = jax.nn.softmax(scores, axis=-1)
    return jnp.einsum('hqk,khd->qhd', low(weights), value_rows, precision=EXACT, preferred_element_type=jnp.float32)

def forward(tokens, params, fragments):
    query_weight, query_bias, key_weight, value_weight, value_bias, out_weight, out_bias, first_gain, first_shift, expand_weight, expand_bias, reduce_weight, reduce_bias, second_gain, second_shift = params
    shaped = (fragments.shape[0], fragments.shape[1], HEADS, HEAD)
    queries = rounded(product(tokens, query_weight) + query_bias).reshape(shaped)
    key_rows = rounded(product(tokens, key_weight)).reshape(shaped)
    value_rows = rounded(product(tokens, value_weight) + value_bias).reshape(shaped)
    checked = jax.checkpoint(attend)
    attended = lax.map(lambda bundle: checked(bundle[0], bundle[1], bundle[2], bundle[3]), (queries, key_rows, value_rows, fragments))
    mixed = rounded(attended.reshape(tokens.shape))
    attention_out = low_back(product(mixed, out_weight) + out_bias)
    hidden = layer_norm(tokens + attention_out, first_gain, first_shift)
    inner = low_back(product(low(hidden), expand_weight) + expand_bias)
    active = low(jax.nn.gelu(inner, approximate=False))
    branch = low_back(product(active, reduce_weight) + reduce_bias)
    return layer_norm(hidden + branch, second_gain, second_shift)

def reference(tokens, segment_ids, query_weight, query_bias, key_weight, value_weight, value_bias, out_weight, out_bias, first_gain, first_shift, expand_weight, expand_bias, reduce_weight, reduce_bias, second_gain, second_shift, cotangent):
    params = tuple((weight.astype(jnp.float32) for weight in (query_weight, query_bias, key_weight, value_weight, value_bias, out_weight, out_bias, first_gain, first_shift, expand_weight, expand_bias, reduce_weight, reduce_bias, second_gain, second_shift)))
    group = math.gcd(SEQS, max(1, 4096 // SEQ_LEN))
    blocks = SEQS // group
    token_groups = tokens.reshape(blocks, group * SEQ_LEN, D)
    fragment_groups = segment_ids.reshape(blocks, group, SEQ_LEN)
    cotangent_groups = cotangent.reshape(blocks, group * SEQ_LEN, D)

    def advance(summed, bundle):
        token_block, fragment_block, cotangent_block = bundle

        def layer(inputs, weights):
            return forward(inputs, weights, fragment_block)
        result, pullback = jax.vjp(layer, token_block.astype(jnp.float32), params)
        input_part, weight_parts = pullback(cotangent_block.astype(jnp.float32))
        summed = jax.tree.map(lambda left, right: left + right, summed, weight_parts)
        return (summed, (result.astype(jnp.bfloat16), input_part))
    start = tuple((jnp.zeros_like(weight) for weight in params))
    gradients, (results, input_parts) = lax.scan(advance, start, (token_groups, fragment_groups, cotangent_groups))
    return (results.reshape(TOKENS, D), input_parts.reshape(TOKENS, D), gradients[0], gradients[1], gradients[2], gradients[3], gradients[4], gradients[5], gradients[6], gradients[7], gradients[8], gradients[9], gradients[10], gradients[11], gradients[12], gradients[13], gradients[14])
```

```python
import jax
import jax.numpy as jnp
from jax import lax
from jax.sharding import PartitionSpec as P

HEADS = 12
HEAD = 64


def layer_norm(rows, gain, shift):
    average = jnp.mean(rows, axis=-1, keepdims=True)
    centered = rows - average
    rescale = lax.rsqrt(jnp.mean(centered * centered, axis=-1, keepdims=True) + 1e-12)
    normed = centered * rescale
    return (normed * gain.astype(jnp.float32) + shift.astype(jnp.float32), normed, rescale)


def norm_back(gradient, normed, rescale, gain):
    scaled = gradient * gain.astype(jnp.float32)
    inner_mean = jnp.mean(scaled * normed, axis=-1, keepdims=True)
    rows_grad = rescale * (scaled - jnp.mean(scaled, axis=-1, keepdims=True) - normed * inner_mean)
    return (rows_grad, jnp.sum(gradient * normed, axis=0), jnp.sum(gradient, axis=0))


def linear(rows, weight, bias):
    return jnp.dot(rows, weight, preferred_element_type=jnp.float32) + bias.astype(jnp.float32)


def weight_grad(rows, gradient):
    return jnp.einsum("ti,to->io", rows, gradient, preferred_element_type=jnp.float32)


def bias_grad(gradient):
    return jnp.sum(gradient.astype(jnp.float32), axis=0)


def back_rows(gradient, weight):
    return jnp.einsum("to,io->ti", gradient, weight, preferred_element_type=jnp.float32)


def gelu_slope(inner):
    normal_cdf = 0.5 * (1.0 + lax.erf(inner * 0.7071067811865476))
    density = jnp.exp(-0.5 * inner * inner) * 0.3989422804014327
    return normal_cdf + inner * density


def masked_scores(queries, key_rows, fragment):
    scaling = queries.shape[-1] ** (-0.5)
    scores = (
        jnp.einsum("qhd,khd->hqk", queries, key_rows, preferred_element_type=jnp.float32) * scaling
    )
    same_fragment = fragment[:, None] == fragment[None, :]
    return jnp.where(same_fragment[None, :, :], scores, -1000000000.0)


def attend_forward(bundle):
    queries, key_rows, value_rows, fragment = bundle
    scores = masked_scores(queries, key_rows, fragment)
    highest = jnp.max(scores, axis=-1, keepdims=True)
    lifted = jnp.exp(scores - highest)
    totals = jnp.sum(lifted, axis=-1, keepdims=True)
    weights = (lifted / totals).astype(jnp.bfloat16)
    mixed = jnp.einsum("hqk,khd->qhd", weights, value_rows, preferred_element_type=jnp.float32)
    return (mixed.astype(jnp.bfloat16), highest + jnp.log(totals))


def attend_backward(bundle):
    queries, key_rows, value_rows, fragment, mixed_grad, log_totals = bundle
    scaling = queries.shape[-1] ** (-0.5)
    weights = jnp.exp(masked_scores(queries, key_rows, fragment) - log_totals)
    value_grad = jnp.einsum(
        "hqk,qhd->khd", weights.astype(jnp.bfloat16), mixed_grad, preferred_element_type=jnp.float32
    )
    prob_grad = jnp.einsum(
        "qhd,khd->hqk", mixed_grad, value_rows, preferred_element_type=jnp.float32
    )
    score_grad = (
        weights * (prob_grad - jnp.sum(prob_grad * weights, axis=-1, keepdims=True))
    ).astype(jnp.bfloat16)
    query_grad = (
        jnp.einsum("hqk,khd->qhd", score_grad, key_rows, preferred_element_type=jnp.float32)
        * scaling
    )
    key_grad = (
        jnp.einsum("hqk,qhd->khd", score_grad, queries, preferred_element_type=jnp.float32)
        * scaling
    )
    return (
        query_grad.astype(jnp.bfloat16),
        key_grad.astype(jnp.bfloat16),
        value_grad.astype(jnp.bfloat16),
    )


def on_device(
    tokens,
    segment_ids,
    query_weight,
    query_bias,
    key_weight,
    value_weight,
    value_bias,
    out_weight,
    out_bias,
    first_gain,
    first_shift,
    expand_weight,
    expand_bias,
    reduce_weight,
    reduce_bias,
    second_gain,
    second_shift,
    cotangent,
):
    seq_count, seq_length = segment_ids.shape
    shaped = (seq_count, seq_length, HEADS, HEAD)
    rows, width = query_weight.shape
    small = (query_bias, value_bias, out_bias, first_gain, first_shift, reduce_bias, second_gain, second_shift)
    small_pack = jnp.concatenate([v[None, :] for v in small] + [expand_bias.reshape(-1, rows)], axis=0)
    gathered_small = lax.all_gather(small_pack, "fsdp", axis=1, tiled=True)
    groups = gathered_small.shape[1] // rows
    vectors = [gathered_small[k] for k in range(8)]
    expand_bias_all = (
        gathered_small[8:].reshape(-1, groups, rows).transpose(1, 0, 2).reshape(groups * expand_bias.shape[0])
    )
    query_bias_all, value_bias_all, out_bias_all, gain1, shift1, reduce_bias_all, gain2, shift2 = vectors
    attention_pack = jnp.stack([query_weight, key_weight, value_weight, out_weight])
    attention_all = lax.all_gather(attention_pack, "fsdp", axis=1, tiled=True)
    expand_all = lax.all_gather(expand_weight, "fsdp", axis=0, tiled=True)
    reduce_all = lax.all_gather(reduce_weight, "fsdp", axis=0, tiled=True)
    wq, wk, wv, wo = attention_all[0], attention_all[1], attention_all[2], attention_all[3]

    queries = linear(tokens, wq, query_bias_all).astype(jnp.bfloat16).reshape(shaped)
    key_rows = jnp.dot(tokens, wk, preferred_element_type=jnp.float32).astype(jnp.bfloat16).reshape(shaped)
    value_rows = linear(tokens, wv, value_bias_all).astype(jnp.bfloat16).reshape(shaped)
    mixed, log_totals = lax.map(attend_forward, (queries, key_rows, value_rows, segment_ids))
    mixed = mixed.reshape(tokens.shape)
    first_sum = tokens.astype(jnp.float32) + linear(mixed, wo, out_bias_all)
    hidden, first_normed, first_rescale = layer_norm(first_sum, gain1, shift1)
    hidden_low = hidden.astype(jnp.bfloat16)
    inner = linear(hidden_low, expand_all, expand_bias_all)
    active = jax.nn.gelu(inner, approximate=False).astype(jnp.bfloat16)
    second_sum = hidden + linear(active, reduce_all, reduce_bias_all)
    output, second_normed, second_rescale = layer_norm(second_sum, gain2, shift2)
    second_grad, grad_second_gain, grad_second_shift = norm_back(
        cotangent.astype(jnp.float32), second_normed, second_rescale, gain2
    )
    branch_grad = second_grad.astype(jnp.bfloat16)
    grad_reduce = weight_grad(active, branch_grad)
    grad_reduce_bias = bias_grad(branch_grad)
    inner_grad = (back_rows(branch_grad, reduce_all) * gelu_slope(inner)).astype(jnp.bfloat16)
    grad_expand = weight_grad(hidden_low, inner_grad)
    grad_expand_bias = bias_grad(inner_grad)
    hidden_grad = second_grad + back_rows(inner_grad, expand_all)
    low = jnp.bfloat16
    scattered_expand = lax.psum_scatter(grad_expand.astype(low), "fsdp", scatter_dimension=0, tiled=True)
    scattered_reduce = lax.psum_scatter(grad_reduce.astype(low), "fsdp", scatter_dimension=0, tiled=True)
    first_grad, grad_first_gain, grad_first_shift = norm_back(
        hidden_grad, first_normed, first_rescale, gain1
    )
    out_grad = first_grad.astype(jnp.bfloat16)
    grad_out = weight_grad(mixed, out_grad)
    grad_out_bias = bias_grad(out_grad)
    mixed_grad = back_rows(out_grad, wo).astype(jnp.bfloat16).reshape(shaped)
    query_grad, key_grad, value_grad = lax.map(
        attend_backward, (queries, key_rows, value_rows, segment_ids, mixed_grad, log_totals)
    )
    query_grad = query_grad.reshape(tokens.shape)
    key_grad = key_grad.reshape(tokens.shape)
    value_grad = value_grad.reshape(tokens.shape)
    grad_query = weight_grad(tokens, query_grad)
    grad_query_bias = bias_grad(query_grad)
    grad_key = weight_grad(tokens, key_grad)
    grad_value = weight_grad(tokens, value_grad)
    grad_value_bias = bias_grad(value_grad)
    input_grad = first_grad + back_rows(query_grad, wq) + back_rows(key_grad, wk) + back_rows(value_grad, wv)
    small_grads = (
        grad_query_bias, grad_value_bias, grad_out_bias, grad_first_gain, grad_first_shift,
        grad_reduce_bias, grad_second_gain, grad_second_shift,
    )
    small_sum = jnp.concatenate(
        [v[None, :] for v in small_grads]
        + [grad_expand_bias.reshape(groups, -1, rows).transpose(1, 0, 2).reshape(-1, groups * rows)],
        axis=0,
    )
    small_sum = lax.psum(small_sum, ("dp", "fsdp"))
    at = lax.axis_index("fsdp") * rows
    small_own = lax.dynamic_slice_in_dim(small_sum, at, rows, axis=1)
    attention_grads = jnp.concatenate([grad_query, grad_key, grad_value, grad_out], axis=1).astype(low)
    attention_own = lax.psum_scatter(attention_grads, "fsdp", scatter_dimension=0, tiled=True)
    attention_own = lax.psum(attention_own, "dp").astype(jnp.float32)
    attention_own = [attention_own[:, k * width : (k + 1) * width] for k in range(4)]
    expand_own = lax.psum(scattered_expand, "dp").astype(jnp.float32)
    reduce_own = lax.psum(scattered_reduce, "dp").astype(jnp.float32)
    return (
        output.astype(jnp.bfloat16),
        input_grad,
        attention_own[0],
        small_own[0],
        attention_own[1],
        attention_own[2],
        small_own[1],
        attention_own[3],
        small_own[2],
        small_own[3],
        small_own[4],
        expand_own,
        small_own[8:].reshape(-1),
        reduce_own,
        small_own[5],
        small_own[6],
        small_own[7],
    )


def solution(mesh):
    in_specs = (
        P(("dp", "fsdp"), None),
        P(("dp", "fsdp"), None),
        P("fsdp", None),
        P("fsdp"),
        P("fsdp", None),
        P("fsdp", None),
        P("fsdp"),
        P("fsdp", None),
        P("fsdp"),
        P("fsdp"),
        P("fsdp"),
        P("fsdp", None),
        P("fsdp"),
        P("fsdp", None),
        P("fsdp"),
        P("fsdp"),
        P("fsdp"),
        P(("dp", "fsdp"), None),
    )
    out_specs = (
        P(("dp", "fsdp"), None),
        P(("dp", "fsdp"), None),
        P("fsdp", None),
        P("fsdp"),
        P("fsdp", None),
        P("fsdp", None),
        P("fsdp"),
        P("fsdp", None),
        P("fsdp"),
        P("fsdp"),
        P("fsdp"),
        P("fsdp", None),
        P("fsdp"),
        P("fsdp", None),
        P("fsdp"),
        P("fsdp"),
        P("fsdp"),
    )
    return jax.shard_map(
        on_device, mesh=mesh, in_specs=in_specs, out_specs=out_specs, check_vma=False
    )
```

```python
import functools

import jax
import jax.numpy as jnp
from jax import lax
from jax.experimental import pallas as pl
from jax.experimental.pallas import tpu as pltpu
from jax.sharding import PartitionSpec as P

HEADS = 12
HEAD = 64
SMALL = 32


def layer_norm(rows, gain, shift):
    average = jnp.mean(rows, axis=-1, keepdims=True)
    centered = rows - average
    rescale = lax.rsqrt(jnp.mean(centered * centered, axis=-1, keepdims=True) + 1e-12)
    normed = centered * rescale
    return (normed * gain.astype(jnp.float32) + shift.astype(jnp.float32), normed, rescale)


def norm_back(gradient, normed, rescale, gain):
    scaled = gradient * gain.astype(jnp.float32)
    inner_mean = jnp.mean(scaled * normed, axis=-1, keepdims=True)
    rows_grad = rescale * (scaled - jnp.mean(scaled, axis=-1, keepdims=True) - normed * inner_mean)
    return (rows_grad, jnp.sum(gradient * normed, axis=0), jnp.sum(gradient, axis=0))


def linear(rows, weight, bias):
    return jnp.dot(rows, weight, preferred_element_type=jnp.float32) + bias.astype(jnp.float32)


def weight_grad(rows, gradient):
    return jnp.einsum("ti,to->io", rows, gradient, preferred_element_type=jnp.float32)


def bias_grad(gradient):
    return jnp.sum(gradient.astype(jnp.float32), axis=0)


def back_rows(gradient, weight):
    return jnp.einsum("to,io->ti", gradient, weight, preferred_element_type=jnp.float32)


def gelu_slope(inner):
    normal_cdf = 0.5 * (1.0 + lax.erf(inner * 0.7071067811865476))
    density = jnp.exp(-0.5 * inner * inner) * 0.3989422804014327
    return normal_cdf + inner * density


def masked_scores(queries, key_rows, fragment):
    scaling = queries.shape[-1] ** (-0.5)
    scores = (
        jnp.einsum("qhd,khd->hqk", queries, key_rows, preferred_element_type=jnp.float32) * scaling
    )
    same_fragment = fragment[:, None] == fragment[None, :]
    return jnp.where(same_fragment[None, :, :], scores, -1000000000.0)


def attend_forward(bundle):
    queries, key_rows, value_rows, fragment = bundle
    scores = masked_scores(queries, key_rows, fragment)
    highest = jnp.max(scores, axis=-1, keepdims=True)
    lifted = jnp.exp(scores - highest)
    totals = jnp.sum(lifted, axis=-1, keepdims=True)
    weights = (lifted / totals).astype(jnp.bfloat16)
    mixed = jnp.einsum("hqk,khd->qhd", weights, value_rows, preferred_element_type=jnp.float32)
    return (mixed.astype(jnp.bfloat16), highest + jnp.log(totals))


def attend_backward(bundle):
    queries, key_rows, value_rows, fragment, mixed_grad, log_totals = bundle
    scaling = queries.shape[-1] ** (-0.5)
    weights = jnp.exp(masked_scores(queries, key_rows, fragment) - log_totals)
    value_grad = jnp.einsum(
        "hqk,qhd->khd", weights.astype(jnp.bfloat16), mixed_grad, preferred_element_type=jnp.float32
    )
    prob_grad = jnp.einsum(
        "qhd,khd->hqk", mixed_grad, value_rows, preferred_element_type=jnp.float32
    )
    score_grad = (
        weights * (prob_grad - jnp.sum(prob_grad * weights, axis=-1, keepdims=True))
    ).astype(jnp.bfloat16)
    query_grad = (
        jnp.einsum("hqk,khd->qhd", score_grad, key_rows, preferred_element_type=jnp.float32)
        * scaling
    )
    key_grad = (
        jnp.einsum("hqk,qhd->khd", score_grad, queries, preferred_element_type=jnp.float32)
        * scaling
    )
    return (
        query_grad.astype(jnp.bfloat16),
        key_grad.astype(jnp.bfloat16),
        value_grad.astype(jnp.bfloat16),
    )


MESH = pl.DeviceIdType.MESH
LINE = 4
ORDER = (3, 0, 2, 1)


def places():
    dp, fs = lax.axis_index("dp"), lax.axis_index("fsdp")
    core, y, z = lax.rem(dp, 2), lax.rem(fs, 2), fs // 2
    return dict(
        core=core, y=y, z=z, fs=fs,
        sibling=(dp + 1 - 2 * core, fs),
        across=(lax.rem(dp + 2, 4), fs),
        side=(dp, fs + 1 - 2 * y),
        up=(dp, fs + 2),
        down=(dp, fs - 2),
    )


def greet(at):
    barrier = pltpu.get_barrier_semaphore()

    def hello(who):
        pl.semaphore_signal(barrier, inc=1, device_id=who, device_id_type=MESH)

    for name in ("sibling", "across", "side"):
        hello(at[name])
    pl.when(at["z"] < LINE - 1)(lambda: hello(at["up"]))
    pl.when(at["z"] > 0)(lambda: hello(at["down"]))
    end = jnp.logical_or(at["z"] == 0, at["z"] == LINE - 1)
    pl.when(end)(lambda: pl.semaphore_wait(barrier, 4))
    pl.when(jnp.logical_not(end))(lambda: pl.semaphore_wait(barrier, 5))


def add_rows(target, *sources):
    rows = target.shape[0]

    def block(k, carry):
        at = pl.ds(pl.multiple_of(k * 16, 16), 16)
        total = sources[0][at, :].astype(jnp.float32)
        for source in sources[1:]:
            total = total + source[at, :].astype(jnp.float32)
        target[at, :] = total.astype(jnp.bfloat16)
        return carry

    lax.fori_loop(0, rows // 16, block, 0)


def scatter_scratch(rows, columns):
    half = rows // 2
    low = jnp.bfloat16
    return [
        pltpu.VMEM((2, LINE, half, columns), low),
        pltpu.VMEM((2, LINE, half, columns), low),
        pltpu.VMEM((LINE, half, columns), low),
        pltpu.VMEM((2, LINE, half, columns), low),
        pltpu.VMEM((half, columns), low),
        pltpu.VMEM((2, half, columns), low),
        pltpu.SemaphoreType.DMA((2,)),
        pltpu.SemaphoreType.DMA((2, 2)),
        pltpu.SemaphoreType.DMA((2, LINE)),
        pltpu.SemaphoreType.DMA((2, 2, LINE)),
        pltpu.SemaphoreType.DMA((2, 2)),
    ]


SCRATCHES = 11


def scatter_events(at, source, out, scratch):
    own, sib, side, line, across, result, load_sem, sib_sem, side_sem, line_sem, last_sem = scratch
    half = own.shape[2]
    core, y, z = at["core"], at["y"], at["z"]
    mine = pl.ds(pl.multiple_of(core * half, 16), half)
    other = pl.ds(pl.multiple_of((1 - core) * half, 16), half)
    column = (1 - y, y)

    def load(k):
        return pltpu.make_async_copy(source.at[:, column[k], mine, :], own.at[k], load_sem.at[k])

    def remote(src, dst, send, recv, who):
        return pltpu.make_async_remote_copy(
            src_ref=src, dst_ref=dst, send_sem=send, recv_sem=recv, device_id=at[who], device_id_type=MESH
        )

    def to_sibling(k):
        return remote(source.at[:, column[k], other, :], sib.at[k], sib_sem.at[0, k], sib_sem.at[1, k], "sibling")

    def to_side(k):
        return remote(own.at[0, k], side.at[k], side_sem.at[0, k], side_sem.at[1, k], "side")

    def to_line(way, k):
        return remote(
            own.at[1, k], line.at[way, k], line_sem.at[0, way, k], line_sem.at[1, way, k], ("up", "down")[way]
        )

    def to_across():
        return remote(own.at[1, z], across, last_sem.at[0, 0], last_sem.at[1, 0], "across")

    def to_last():
        return remote(result.at[core], result.at[core], last_sem.at[0, 1], last_sem.at[1, 1], "sibling")

    def begin():
        for k in range(2):
            to_sibling(k).start()
            load(k).start()

    def first():
        load(0).wait()
        to_sibling(0).wait_recv()
        for k in ORDER:
            add_rows(own.at[0, k], own.at[0, k], sib.at[0, k])
            to_side(k).start()
        load(1).wait()
        to_sibling(1).wait_recv()
        for k in ORDER:
            add_rows(own.at[1, k], own.at[1, k], sib.at[1, k])

    def chain(k):
        to_side(k).wait_recv()

        def pass_on(way, inner):
            @pl.when(inner)
            def _():
                to_line(way, k).wait_recv()
                add_rows(own.at[1, k], own.at[1, k], side.at[k], line.at[way, k])

            @pl.when(jnp.logical_not(inner))
            def _():
                add_rows(own.at[1, k], own.at[1, k], side.at[k])

            to_line(way, k).start()

        pl.when(k > z)(lambda: pass_on(0, z > 0))
        pl.when(k < z)(lambda: pass_on(1, z < LINE - 1))
        pl.when(k == z)(lambda: add_rows(own.at[1, k], own.at[1, k], side.at[k]))

    def gather_line():
        for k in range(LINE):

            @pl.when(k == z)
            def _():
                parts = []
                if k > 0:
                    to_line(0, k).wait_recv()
                    parts.append(line.at[0, k])
                if k < LINE - 1:
                    to_line(1, k).wait_recv()
                    parts.append(line.at[1, k])
                add_rows(own.at[1, k], own.at[1, k], *parts)

        to_across().start()

    def finish():
        to_across().wait_recv()
        add_rows(result.at[core], own.at[1, z], across)
        to_last().start()

    def drain():
        to_last().wait_recv()
        out[0:half, :] = result[0]
        out[half : 2 * half, :] = result[1]
        to_last().wait_send()
        to_across().wait_send()
        for k in range(2):
            to_sibling(k).wait_send()
        for k in range(LINE):
            to_side(k).wait_send()
            pl.when(k > z)(lambda: to_line(0, k).wait_send())
            pl.when(k < z)(lambda: to_line(1, k).wait_send())

    chains = [functools.partial(chain, k) for k in ORDER]
    return begin, first, chains, gather_line, finish, drain


def scatter_kernel(count, *refs):
    sources, outs, scratch = refs[:count], refs[count : 2 * count], refs[2 * count :]
    at = places()
    greet(at)
    parts = [
        scatter_events(at, sources[g], outs[g], scratch[g * SCRATCHES : (g + 1) * SCRATCHES]) for g in range(count)
    ]
    for begin, *_ in parts:
        begin()
    for _, first, *_ in parts:
        first()
    for _, _, chains, *_ in parts:
        for step in chains:
            step()
    for part in parts:
        part[3]()
    for part in parts:
        part[4]()
    for part in parts:
        part[5]()


def scatter_all(sources, ident):
    shapes = [s.shape[2:] for s in sources]
    return pl.pallas_call(
        functools.partial(scatter_kernel, len(sources)),
        out_shape=[jax.ShapeDtypeStruct(s, jnp.bfloat16) for s in shapes],
        in_specs=[pl.BlockSpec(memory_space=pl.ANY)] * len(sources),
        out_specs=[pl.BlockSpec(memory_space=pltpu.VMEM)] * len(sources),
        scratch_shapes=[x for s in shapes for x in scatter_scratch(*s)],
        compiler_params=pltpu.CompilerParams(
            collective_id=ident, has_side_effects=True, vmem_limit_bytes=60 * 1024 * 1024
        ),
        name="scatter_sum",
    )(*sources)


def gather_scratch():
    return [pltpu.SemaphoreType.DMA((2 * LINE, 2)), pltpu.SemaphoreType.DMA((2 * LINE, 4))]


def gather_events(at, shard, whole, scratch):
    arrived, sent = scratch
    half = shard.shape[0] // 2
    core, y, z, me = at["core"], at["y"], at["z"], at["fs"]
    mine = pl.ds(pl.multiple_of(core * half, 16), half)
    ways = ("side", "up", "down")

    def pass_on(src, owner, way):
        return pltpu.make_async_remote_copy(
            src_ref=src,
            dst_ref=whole.at[owner, mine, :],
            send_sem=sent.at[owner, way],
            recv_sem=arrived.at[owner, core],
            device_id=at[ways[way]],
            device_id_type=MESH,
        )

    def half_to_sibling(owner):
        return pltpu.make_async_remote_copy(
            src_ref=whole.at[owner, mine, :],
            dst_ref=whole.at[owner, mine, :],
            send_sem=sent.at[owner, 3],
            recv_sem=arrived.at[owner, core],
            device_id=at["sibling"],
            device_id_type=MESH,
        )

    def half_from_sibling(owner):
        theirs = pl.ds(pl.multiple_of((1 - core) * half, 16), half)
        return pltpu.make_async_remote_copy(
            src_ref=whole.at[owner, theirs, :],
            dst_ref=whole.at[owner, theirs, :],
            send_sem=sent.at[owner, 3],
            recv_sem=arrived.at[owner, 1 - core],
            device_id=at["sibling"],
            device_id_type=MESH,
        )

    def own_to_sibling():
        return pltpu.make_async_remote_copy(
            src_ref=shard,
            dst_ref=whole.at[me],
            send_sem=sent.at[me, 3],
            recv_sem=arrived.at[me, 0],
            device_id=at["sibling"],
            device_id_type=MESH,
        )

    def begin():
        src = shard.at[mine, :]
        pl.when(z < LINE - 1)(lambda: pass_on(src, me, 1).start())
        pl.when(z > 0)(lambda: pass_on(src, me, 2).start())
        pass_on(src, me, 0).start()
        own_to_sibling().start()

    def relay(t, sign):
        owner = me + 2 * t * sign

        @pl.when((z - t >= 0) if sign < 0 else (z + t <= LINE - 1))
        def _():
            held = whole.at[owner, mine, :]
            pass_on(held, owner, 0).wait_recv()
            if sign < 0:
                pl.when(z < LINE - 1)(lambda: pass_on(held, owner, 1).start())
            else:
                pl.when(z > 0)(lambda: pass_on(held, owner, 2).start())
            pass_on(held, owner, 0).start()
            half_to_sibling(owner).start()

    def from_side(t, sign):
        owner = me + 1 - 2 * y + 2 * t * sign

        @pl.when((z - t >= 0) if sign < 0 else (z + t <= LINE - 1))
        def _():
            pass_on(whole.at[owner, mine, :], owner, 0).wait_recv()
            half_to_sibling(owner).start()

    def settle():
        own_to_sibling().wait_recv()
        for owner in range(2 * LINE):
            pl.when(owner != me)(lambda: half_from_sibling(owner).wait_recv())

    def drain():
        own_to_sibling().wait_send()
        src = shard.at[mine, :]
        for owner in range(2 * LINE):
            line = owner // 2
            same = owner % 2 == y

            @pl.when(same)
            def _():
                pass_on(src, owner, 0).wait_send()
                pl.when(jnp.logical_and(line <= z, z < LINE - 1))(lambda: pass_on(src, owner, 1).wait_send())
                pl.when(jnp.logical_and(line >= z, z > 0))(lambda: pass_on(src, owner, 2).wait_send())

            pl.when(owner != me)(lambda: half_to_sibling(owner).wait_send())

    relays = [functools.partial(relay, t, s) for t in range(1, LINE) for s in (-1, 1)]
    sides = [functools.partial(from_side, 0, 1)]
    sides += [functools.partial(from_side, t, s) for t in range(1, LINE) for s in (-1, 1)]
    return begin, relays, sides, settle, drain


def gather_kernel(count, *refs):
    shards, wholes, scratch = refs[:count], refs[count : 2 * count], refs[2 * count :]
    at = places()
    greet(at)
    parts = [gather_events(at, shards[g], wholes[g], scratch[2 * g : 2 * g + 2]) for g in range(count)]
    for begin, *_ in parts:
        begin()
    for _, relays, sides, *_ in parts:
        for step in relays:
            step()
    for _, relays, sides, *_ in parts:
        for step in sides:
            step()
    for part in parts:
        part[3]()
        part[4]()


def gather_all(shards, ident):
    return pl.pallas_call(
        functools.partial(gather_kernel, len(shards)),
        out_shape=[jax.ShapeDtypeStruct((2 * LINE, *s.shape), jnp.bfloat16) for s in shards],
        in_specs=[pl.BlockSpec(memory_space=pltpu.VMEM)] * len(shards),
        out_specs=[pl.BlockSpec(memory_space=pltpu.VMEM)] * len(shards),
        scratch_shapes=[x for s in shards for x in gather_scratch()],
        compiler_params=pltpu.CompilerParams(collective_id=ident, has_side_effects=True, vmem_limit_bytes=60 * 1024 * 1024),
        name="gather",
    )(*shards)


def plain_on_device(
    tokens,
    segment_ids,
    query_weight,
    query_bias,
    key_weight,
    value_weight,
    value_bias,
    out_weight,
    out_bias,
    first_gain,
    first_shift,
    expand_weight,
    expand_bias,
    reduce_weight,
    reduce_bias,
    second_gain,
    second_shift,
    cotangent,
):
    seq_count, seq_length = segment_ids.shape
    shaped = (seq_count, seq_length, HEADS, HEAD)
    rows, width = query_weight.shape
    small = (query_bias, value_bias, out_bias, first_gain, first_shift, reduce_bias, second_gain, second_shift)
    small_pack = jnp.concatenate([v[None, :] for v in small] + [expand_bias.reshape(-1, rows)], axis=0)
    gathered_small = lax.all_gather(small_pack, "fsdp", axis=1, tiled=True)
    groups = gathered_small.shape[1] // rows
    vectors = [gathered_small[k] for k in range(8)]
    expand_bias_all = (
        gathered_small[8:].reshape(-1, groups, rows).transpose(1, 0, 2).reshape(groups * expand_bias.shape[0])
    )
    query_bias_all, value_bias_all, out_bias_all, gain1, shift1, reduce_bias_all, gain2, shift2 = vectors
    attention_pack = jnp.stack([query_weight, key_weight, value_weight, out_weight])
    attention_all = lax.all_gather(attention_pack, "fsdp", axis=1, tiled=True)
    expand_all = lax.all_gather(expand_weight, "fsdp", axis=0, tiled=True)
    reduce_all = lax.all_gather(reduce_weight, "fsdp", axis=0, tiled=True)
    wq, wk, wv, wo = attention_all[0], attention_all[1], attention_all[2], attention_all[3]

    queries = linear(tokens, wq, query_bias_all).astype(jnp.bfloat16).reshape(shaped)
    key_rows = jnp.dot(tokens, wk, preferred_element_type=jnp.float32).astype(jnp.bfloat16).reshape(shaped)
    value_rows = linear(tokens, wv, value_bias_all).astype(jnp.bfloat16).reshape(shaped)
    mixed, log_totals = lax.map(attend_forward, (queries, key_rows, value_rows, segment_ids))
    mixed = mixed.reshape(tokens.shape)
    first_sum = tokens.astype(jnp.float32) + linear(mixed, wo, out_bias_all)
    hidden, first_normed, first_rescale = layer_norm(first_sum, gain1, shift1)
    hidden_low = hidden.astype(jnp.bfloat16)
    inner = linear(hidden_low, expand_all, expand_bias_all)
    active = jax.nn.gelu(inner, approximate=False).astype(jnp.bfloat16)
    second_sum = hidden + linear(active, reduce_all, reduce_bias_all)
    output, second_normed, second_rescale = layer_norm(second_sum, gain2, shift2)
    second_grad, grad_second_gain, grad_second_shift = norm_back(
        cotangent.astype(jnp.float32), second_normed, second_rescale, gain2
    )
    branch_grad = second_grad.astype(jnp.bfloat16)
    grad_reduce = weight_grad(active, branch_grad)
    grad_reduce_bias = bias_grad(branch_grad)
    inner_grad = (back_rows(branch_grad, reduce_all) * gelu_slope(inner)).astype(jnp.bfloat16)
    grad_expand = weight_grad(hidden_low, inner_grad)
    grad_expand_bias = bias_grad(inner_grad)
    hidden_grad = second_grad + back_rows(inner_grad, expand_all)
    low = jnp.bfloat16
    scattered_expand = lax.psum_scatter(grad_expand.astype(low), "fsdp", scatter_dimension=0, tiled=True)
    scattered_reduce = lax.psum_scatter(grad_reduce.astype(low), "fsdp", scatter_dimension=0, tiled=True)
    first_grad, grad_first_gain, grad_first_shift = norm_back(
        hidden_grad, first_normed, first_rescale, gain1
    )
    out_grad = first_grad.astype(jnp.bfloat16)
    grad_out = weight_grad(mixed, out_grad)
    grad_out_bias = bias_grad(out_grad)
    mixed_grad = back_rows(out_grad, wo).astype(jnp.bfloat16).reshape(shaped)
    query_grad, key_grad, value_grad = lax.map(
        attend_backward, (queries, key_rows, value_rows, segment_ids, mixed_grad, log_totals)
    )
    query_grad = query_grad.reshape(tokens.shape)
    key_grad = key_grad.reshape(tokens.shape)
    value_grad = value_grad.reshape(tokens.shape)
    grad_query = weight_grad(tokens, query_grad)
    grad_query_bias = bias_grad(query_grad)
    grad_key = weight_grad(tokens, key_grad)
    grad_value = weight_grad(tokens, value_grad)
    grad_value_bias = bias_grad(value_grad)
    input_grad = first_grad + back_rows(query_grad, wq) + back_rows(key_grad, wk) + back_rows(value_grad, wv)
    small_grads = (
        grad_query_bias, grad_value_bias, grad_out_bias, grad_first_gain, grad_first_shift,
        grad_reduce_bias, grad_second_gain, grad_second_shift,
    )
    small_sum = jnp.concatenate(
        [v[None, :] for v in small_grads]
        + [grad_expand_bias.reshape(groups, -1, rows).transpose(1, 0, 2).reshape(-1, groups * rows)],
        axis=0,
    )
    small_sum = lax.psum(small_sum, ("dp", "fsdp"))
    at = lax.axis_index("fsdp") * rows
    small_own = lax.dynamic_slice_in_dim(small_sum, at, rows, axis=1)
    attention_grads = jnp.concatenate([grad_query, grad_key, grad_value, grad_out], axis=1).astype(low)
    attention_own = lax.psum_scatter(attention_grads, "fsdp", scatter_dimension=0, tiled=True)
    attention_own = lax.psum(attention_own, "dp").astype(jnp.float32)
    attention_own = [attention_own[:, k * width : (k + 1) * width] for k in range(4)]
    expand_own = lax.psum(scattered_expand, "dp").astype(jnp.float32)
    reduce_own = lax.psum(scattered_reduce, "dp").astype(jnp.float32)
    return (
        output.astype(jnp.bfloat16),
        input_grad,
        attention_own[0],
        small_own[0],
        attention_own[1],
        attention_own[2],
        small_own[1],
        attention_own[3],
        small_own[2],
        small_own[3],
        small_own[4],
        expand_own,
        small_own[8:].reshape(-1),
        reduce_own,
        small_own[5],
        small_own[6],
        small_own[7],
    )


def on_device(
    tokens,
    segment_ids,
    query_weight,
    query_bias,
    key_weight,
    value_weight,
    value_bias,
    out_weight,
    out_bias,
    first_gain,
    first_shift,
    expand_weight,
    expand_bias,
    reduce_weight,
    reduce_bias,
    second_gain,
    second_shift,
    cotangent,
):
    seq_count, seq_length = segment_ids.shape
    shaped = (seq_count, seq_length, HEADS, HEAD)
    rows, width = query_weight.shape
    low = jnp.bfloat16
    me = lax.axis_index("fsdp")
    shards = 2 * LINE
    vectors = jnp.stack(
        [query_bias, value_bias, out_bias, first_gain, first_shift, reduce_bias, second_gain, second_shift]
    )
    count = expand_bias.shape[0]
    per_row = width // count
    small = lax.dynamic_update_slice(jnp.zeros((SMALL, width), low), vectors, (0, me * rows))
    small = lax.dynamic_update_slice(small, expand_bias[None, :], (8 + me // per_row, lax.rem(me, per_row) * count))
    pack = jnp.concatenate([query_weight, key_weight, value_weight, out_weight, small], axis=0)
    (attention_all,) = gather_all([pack], 0)
    wq, wk, wv, wo = [attention_all[:, k * rows : (k + 1) * rows].reshape(width, width) for k in range(4)]
    small_all = jnp.sum(attention_all[:, 4 * rows :].astype(jnp.float32), axis=0)
    query_bias_all, value_bias_all, out_bias_all, gain1, shift1, reduce_bias_all, gain2, shift2 = [
        small_all[k] for k in range(8)
    ]
    expand_bias_all = small_all[8 : 8 + shards // per_row].reshape(-1)
    expand_all, reduce_all = gather_all([expand_weight, reduce_weight], 1)
    expand_all = expand_all.reshape(width, -1)
    reduce_all = reduce_all.reshape(-1, width)

    queries = linear(tokens, wq, query_bias_all).astype(jnp.bfloat16).reshape(shaped)
    key_rows = jnp.dot(tokens, wk, preferred_element_type=jnp.float32).astype(jnp.bfloat16).reshape(shaped)
    value_rows = linear(tokens, wv, value_bias_all).astype(jnp.bfloat16).reshape(shaped)
    mixed, log_totals = lax.map(attend_forward, (queries, key_rows, value_rows, segment_ids))
    mixed = mixed.reshape(tokens.shape)
    first_sum = tokens.astype(jnp.float32) + linear(mixed, wo, out_bias_all)
    hidden, first_normed, first_rescale = layer_norm(first_sum, gain1, shift1)
    hidden_low = hidden.astype(jnp.bfloat16)
    inner = linear(hidden_low, expand_all, expand_bias_all)
    active = jax.nn.gelu(inner, approximate=False).astype(jnp.bfloat16)
    second_sum = hidden + linear(active, reduce_all, reduce_bias_all)
    output, second_normed, second_rescale = layer_norm(second_sum, gain2, shift2)
    second_grad, grad_second_gain, grad_second_shift = norm_back(
        cotangent.astype(jnp.float32), second_normed, second_rescale, gain2
    )
    branch_grad = second_grad.astype(jnp.bfloat16)
    grad_reduce = weight_grad(active, branch_grad)
    grad_reduce_bias = bias_grad(branch_grad)
    inner_grad = (back_rows(branch_grad, reduce_all) * gelu_slope(inner)).astype(jnp.bfloat16)
    grad_expand = weight_grad(hidden_low, inner_grad)
    grad_expand_bias = bias_grad(inner_grad)
    hidden_grad = second_grad + back_rows(inner_grad, expand_all)
    expand_own, reduce_own = scatter_all(
        [
            grad_expand.astype(low).reshape(LINE, 2, rows, -1),
            grad_reduce.astype(low).reshape(LINE, 2, -1, width),
        ],
        2,
    )
    first_grad, grad_first_gain, grad_first_shift = norm_back(
        hidden_grad, first_normed, first_rescale, gain1
    )
    out_grad = first_grad.astype(jnp.bfloat16)
    grad_out = weight_grad(mixed, out_grad)
    grad_out_bias = bias_grad(out_grad)
    mixed_grad = back_rows(out_grad, wo).astype(jnp.bfloat16).reshape(shaped)
    query_grad, key_grad, value_grad = lax.map(
        attend_backward, (queries, key_rows, value_rows, segment_ids, mixed_grad, log_totals)
    )
    query_grad = query_grad.reshape(tokens.shape)
    key_grad = key_grad.reshape(tokens.shape)
    value_grad = value_grad.reshape(tokens.shape)
    grad_query = weight_grad(tokens, query_grad)
    grad_query_bias = bias_grad(query_grad)
    grad_key = weight_grad(tokens, key_grad)
    grad_value = weight_grad(tokens, value_grad)
    grad_value_bias = bias_grad(value_grad)
    input_grad = first_grad + back_rows(query_grad, wq) + back_rows(key_grad, wk) + back_rows(value_grad, wv)
    small_grads = (
        grad_query_bias, grad_value_bias, grad_out_bias, grad_first_gain, grad_first_shift,
        grad_reduce_bias, grad_second_gain, grad_second_shift,
    )
    small_grads = jnp.stack(small_grads).reshape(8, shards, rows).transpose(1, 0, 2)
    small_grads = jnp.concatenate([small_grads, grad_expand_bias.reshape(shards, -1, rows)], axis=1)
    small_grads = jnp.pad(
        small_grads.astype(low), ((0, 0), (0, SMALL - small_grads.shape[1]), (0, width - rows))
    )
    attention_grads = jnp.concatenate(
        [g.astype(low).reshape(shards, rows, width) for g in (grad_query, grad_key, grad_value, grad_out)]
        + [small_grads],
        axis=1,
    )
    (attention_own,) = scatter_all([attention_grads.reshape(LINE, 2, -1, width)], 3)
    attention_own = attention_own.astype(jnp.float32)
    small_own = attention_own[4 * rows :, :rows]
    attention_own = [attention_own[k * rows : (k + 1) * rows] for k in range(4)]
    return (
        output.astype(low),
        input_grad,
        attention_own[0],
        small_own[0],
        attention_own[1],
        attention_own[2],
        small_own[1],
        attention_own[3],
        small_own[2],
        small_own[3],
        small_own[4],
        expand_own.astype(jnp.float32),
        small_own[8 : 8 + count // rows].reshape(-1),
        reduce_own.astype(jnp.float32),
        small_own[5],
        small_own[6],
        small_own[7],
    )


def solution(mesh):
    fits = mesh.shape["fsdp"] == 2 * LINE and mesh.shape["dp"] == 4
    body = on_device if fits else plain_on_device
    in_specs = (
        P(("dp", "fsdp"), None),
        P(("dp", "fsdp"), None),
        P("fsdp", None),
        P("fsdp"),
        P("fsdp", None),
        P("fsdp", None),
        P("fsdp"),
        P("fsdp", None),
        P("fsdp"),
        P("fsdp"),
        P("fsdp"),
        P("fsdp", None),
        P("fsdp"),
        P("fsdp", None),
        P("fsdp"),
        P("fsdp"),
        P("fsdp"),
        P(("dp", "fsdp"), None),
    )
    out_specs = (
        P(("dp", "fsdp"), None),
        P(("dp", "fsdp"), None),
        P("fsdp", None),
        P("fsdp"),
        P("fsdp", None),
        P("fsdp", None),
        P("fsdp"),
        P("fsdp", None),
        P("fsdp"),
        P("fsdp"),
        P("fsdp"),
        P("fsdp", None),
        P("fsdp"),
        P("fsdp", None),
        P("fsdp"),
        P("fsdp"),
        P("fsdp"),
    )
    return jax.shard_map(
        body, mesh=mesh, in_specs=in_specs, out_specs=out_specs, check_vma=False
    )
```

```python
import functools

import jax
import jax.numpy as jnp
from jax import lax
from jax.experimental import pallas as pl
from jax.experimental.pallas import tpu as pltpu
from jax.sharding import PartitionSpec as P

HEADS = 12
HEAD = 64
SMALL = 32


def layer_norm(rows, gain, shift):
    average = jnp.mean(rows, axis=-1, keepdims=True)
    centered = rows - average
    rescale = lax.rsqrt(jnp.mean(centered * centered, axis=-1, keepdims=True) + 1e-12)
    normed = centered * rescale
    return (normed * gain.astype(jnp.float32) + shift.astype(jnp.float32), normed, rescale)


def norm_back(gradient, normed, rescale, gain):
    scaled = gradient * gain.astype(jnp.float32)
    inner_mean = jnp.mean(scaled * normed, axis=-1, keepdims=True)
    rows_grad = rescale * (scaled - jnp.mean(scaled, axis=-1, keepdims=True) - normed * inner_mean)
    return (rows_grad, jnp.sum(gradient * normed, axis=0), jnp.sum(gradient, axis=0))


def linear(rows, weight, bias):
    return jnp.dot(rows, weight, preferred_element_type=jnp.float32) + bias.astype(jnp.float32)


def weight_grad(rows, gradient):
    return jnp.einsum("ti,to->io", rows, gradient, preferred_element_type=jnp.float32)


def bias_grad(gradient):
    return jnp.sum(gradient.astype(jnp.float32), axis=0)


def back_rows(gradient, weight):
    return jnp.einsum("to,io->ti", gradient, weight, preferred_element_type=jnp.float32)


def gelu_slope(inner):
    normal_cdf = 0.5 * (1.0 + lax.erf(inner * 0.7071067811865476))
    density = jnp.exp(-0.5 * inner * inner) * 0.3989422804014327
    return normal_cdf + inner * density


def masked_scores(queries, key_rows, fragment):
    scaling = queries.shape[-1] ** (-0.5)
    scores = (
        jnp.einsum("qhd,khd->hqk", queries, key_rows, preferred_element_type=jnp.float32) * scaling
    )
    same_fragment = fragment[:, None] == fragment[None, :]
    return jnp.where(same_fragment[None, :, :], scores, -1000000000.0)


def attend_forward(bundle):
    queries, key_rows, value_rows, fragment = bundle
    scores = masked_scores(queries, key_rows, fragment)
    highest = jnp.max(scores, axis=-1, keepdims=True)
    lifted = jnp.exp(scores - highest)
    totals = jnp.sum(lifted, axis=-1, keepdims=True)
    weights = (lifted / totals).astype(jnp.bfloat16)
    mixed = jnp.einsum("hqk,khd->qhd", weights, value_rows, preferred_element_type=jnp.float32)
    return (mixed.astype(jnp.bfloat16), highest + jnp.log(totals))


def attend_backward(bundle):
    queries, key_rows, value_rows, fragment, mixed_grad, log_totals = bundle
    scaling = queries.shape[-1] ** (-0.5)
    weights = jnp.exp(masked_scores(queries, key_rows, fragment) - log_totals)
    value_grad = jnp.einsum(
        "hqk,qhd->khd", weights.astype(jnp.bfloat16), mixed_grad, preferred_element_type=jnp.float32
    )
    prob_grad = jnp.einsum(
        "qhd,khd->hqk", mixed_grad, value_rows, preferred_element_type=jnp.float32
    )
    score_grad = (
        weights * (prob_grad - jnp.sum(prob_grad * weights, axis=-1, keepdims=True))
    ).astype(jnp.bfloat16)
    query_grad = (
        jnp.einsum("hqk,khd->qhd", score_grad, key_rows, preferred_element_type=jnp.float32)
        * scaling
    )
    key_grad = (
        jnp.einsum("hqk,qhd->khd", score_grad, queries, preferred_element_type=jnp.float32)
        * scaling
    )
    return (
        query_grad.astype(jnp.bfloat16),
        key_grad.astype(jnp.bfloat16),
        value_grad.astype(jnp.bfloat16),
    )


MESH = pl.DeviceIdType.MESH
LINE = 4
ORDER = (3, 0, 2, 1)


def places():
    dp, fs = lax.axis_index("dp"), lax.axis_index("fsdp")
    core, y, z = lax.rem(dp, 2), lax.rem(fs, 2), fs // 2
    return dict(
        core=core, y=y, z=z, fs=fs,
        sibling=(dp + 1 - 2 * core, fs),
        across=(lax.rem(dp + 2, 4), fs),
        side=(dp, fs + 1 - 2 * y),
        up=(dp, fs + 2),
        down=(dp, fs - 2),
    )


def greet(at):
    barrier = pltpu.get_barrier_semaphore()

    def hello(who):
        pl.semaphore_signal(barrier, inc=1, device_id=who, device_id_type=MESH)

    for name in ("sibling", "across", "side"):
        hello(at[name])
    pl.when(at["z"] < LINE - 1)(lambda: hello(at["up"]))
    pl.when(at["z"] > 0)(lambda: hello(at["down"]))
    end = jnp.logical_or(at["z"] == 0, at["z"] == LINE - 1)
    pl.when(end)(lambda: pl.semaphore_wait(barrier, 4))
    pl.when(jnp.logical_not(end))(lambda: pl.semaphore_wait(barrier, 5))


def add_rows(target, *sources):
    rows = target.shape[0]

    def block(k, carry):
        at = pl.ds(pl.multiple_of(k * 16, 16), 16)
        total = sources[0][at, :].astype(jnp.float32)
        for source in sources[1:]:
            total = total + source[at, :].astype(jnp.float32)
        target[at, :] = total.astype(jnp.bfloat16)
        return carry

    lax.fori_loop(0, rows // 16, block, 0)


def scatter_scratch(rows, columns):
    half = rows // 2
    low = jnp.bfloat16
    return [
        pltpu.VMEM((2, LINE, half, columns), low),
        pltpu.VMEM((2, LINE, half, columns), low),
        pltpu.VMEM((LINE, half, columns), low),
        pltpu.VMEM((2, LINE, half, columns), low),
        pltpu.VMEM((half, columns), low),
        pltpu.VMEM((2, half, columns), low),
        pltpu.SemaphoreType.DMA((2,)),
        pltpu.SemaphoreType.DMA((2, 2)),
        pltpu.SemaphoreType.DMA((2, LINE)),
        pltpu.SemaphoreType.DMA((2, 2, LINE)),
        pltpu.SemaphoreType.DMA((2, 2)),
    ]


SCRATCHES = 11


def scatter_events(at, source, out, scratch):
    own, sib, side, line, across, result, load_sem, sib_sem, side_sem, line_sem, last_sem = scratch
    half = own.shape[2]
    core, y, z = at["core"], at["y"], at["z"]
    mine = pl.ds(pl.multiple_of(core * half, 16), half)
    other = pl.ds(pl.multiple_of((1 - core) * half, 16), half)
    column = (1 - y, y)

    def load(k):
        return pltpu.make_async_copy(source.at[:, column[k], mine, :], own.at[k], load_sem.at[k])

    def remote(src, dst, send, recv, who):
        return pltpu.make_async_remote_copy(
            src_ref=src, dst_ref=dst, send_sem=send, recv_sem=recv, device_id=at[who], device_id_type=MESH
        )

    def to_sibling(k):
        return remote(source.at[:, column[k], other, :], sib.at[k], sib_sem.at[0, k], sib_sem.at[1, k], "sibling")

    def to_side(k):
        return remote(own.at[0, k], side.at[k], side_sem.at[0, k], side_sem.at[1, k], "side")

    def to_line(way, k):
        return remote(
            own.at[1, k], line.at[way, k], line_sem.at[0, way, k], line_sem.at[1, way, k], ("up", "down")[way]
        )

    def to_across():
        return remote(own.at[1, z], across, last_sem.at[0, 0], last_sem.at[1, 0], "across")

    def to_last():
        return remote(result.at[core], result.at[core], last_sem.at[0, 1], last_sem.at[1, 1], "sibling")

    def begin():
        for k in range(2):
            to_sibling(k).start()
            load(k).start()

    def first():
        load(0).wait()
        to_sibling(0).wait_recv()
        for k in ORDER:
            add_rows(own.at[0, k], own.at[0, k], sib.at[0, k])
            to_side(k).start()
        load(1).wait()
        to_sibling(1).wait_recv()
        for k in ORDER:
            add_rows(own.at[1, k], own.at[1, k], sib.at[1, k])

    def chain(k):
        to_side(k).wait_recv()

        def pass_on(way, inner):
            @pl.when(inner)
            def _():
                to_line(way, k).wait_recv()
                add_rows(own.at[1, k], own.at[1, k], side.at[k], line.at[way, k])

            @pl.when(jnp.logical_not(inner))
            def _():
                add_rows(own.at[1, k], own.at[1, k], side.at[k])

            to_line(way, k).start()

        pl.when(k > z)(lambda: pass_on(0, z > 0))
        pl.when(k < z)(lambda: pass_on(1, z < LINE - 1))
        pl.when(k == z)(lambda: add_rows(own.at[1, k], own.at[1, k], side.at[k]))

    def gather_line():
        for k in range(LINE):

            @pl.when(k == z)
            def _():
                parts = []
                if k > 0:
                    to_line(0, k).wait_recv()
                    parts.append(line.at[0, k])
                if k < LINE - 1:
                    to_line(1, k).wait_recv()
                    parts.append(line.at[1, k])
                add_rows(own.at[1, k], own.at[1, k], *parts)

        to_across().start()

    def finish():
        to_across().wait_recv()
        add_rows(result.at[core], own.at[1, z], across)
        to_last().start()

    def drain():
        to_last().wait_recv()
        out[0:half, :] = result[0]
        out[half : 2 * half, :] = result[1]
        to_last().wait_send()
        to_across().wait_send()
        for k in range(2):
            to_sibling(k).wait_send()
        for k in range(LINE):
            to_side(k).wait_send()
            pl.when(k > z)(lambda: to_line(0, k).wait_send())
            pl.when(k < z)(lambda: to_line(1, k).wait_send())

    chains = [functools.partial(chain, k) for k in ORDER]
    return begin, first, chains, gather_line, finish, drain


def scatter_kernel(count, *refs):
    sources, outs, scratch = refs[:count], refs[count : 2 * count], refs[2 * count :]
    at = places()
    greet(at)
    parts = [
        scatter_events(at, sources[g], outs[g], scratch[g * SCRATCHES : (g + 1) * SCRATCHES]) for g in range(count)
    ]
    for begin, *_ in parts:
        begin()
    for _, first, *_ in parts:
        first()
    for _, _, chains, *_ in parts:
        for step in chains:
            step()
    for part in parts:
        part[3]()
    for part in parts:
        part[4]()
    for part in parts:
        part[5]()


def scatter_all(sources, ident):
    shapes = [s.shape[2:] for s in sources]
    return pl.pallas_call(
        functools.partial(scatter_kernel, len(sources)),
        out_shape=[jax.ShapeDtypeStruct(s, jnp.bfloat16) for s in shapes],
        in_specs=[pl.BlockSpec(memory_space=pl.ANY)] * len(sources),
        out_specs=[pl.BlockSpec(memory_space=pltpu.VMEM)] * len(sources),
        scratch_shapes=[x for s in shapes for x in scatter_scratch(*s)],
        compiler_params=pltpu.CompilerParams(
            collective_id=ident, has_side_effects=True, vmem_limit_bytes=60 * 1024 * 1024
        ),
        name="scatter_sum",
    )(*sources)


def gather_scratch():
    return [pltpu.SemaphoreType.DMA((2 * LINE, 2)), pltpu.SemaphoreType.DMA((2 * LINE, 4))]


def gather_events(at, shard, whole, scratch):
    arrived, sent = scratch
    half = shard.shape[0] // 2
    core, y, z, me = at["core"], at["y"], at["z"], at["fs"]
    mine = pl.ds(pl.multiple_of(core * half, 16), half)
    ways = ("side", "up", "down")

    def pass_on(src, owner, way):
        return pltpu.make_async_remote_copy(
            src_ref=src,
            dst_ref=whole.at[owner, mine, :],
            send_sem=sent.at[owner, way],
            recv_sem=arrived.at[owner, core],
            device_id=at[ways[way]],
            device_id_type=MESH,
        )

    def half_to_sibling(owner):
        return pltpu.make_async_remote_copy(
            src_ref=whole.at[owner, mine, :],
            dst_ref=whole.at[owner, mine, :],
            send_sem=sent.at[owner, 3],
            recv_sem=arrived.at[owner, core],
            device_id=at["sibling"],
            device_id_type=MESH,
        )

    def half_from_sibling(owner):
        theirs = pl.ds(pl.multiple_of((1 - core) * half, 16), half)
        return pltpu.make_async_remote_copy(
            src_ref=whole.at[owner, theirs, :],
            dst_ref=whole.at[owner, theirs, :],
            send_sem=sent.at[owner, 3],
            recv_sem=arrived.at[owner, 1 - core],
            device_id=at["sibling"],
            device_id_type=MESH,
        )

    def own_to_sibling():
        return pltpu.make_async_remote_copy(
            src_ref=shard,
            dst_ref=whole.at[me],
            send_sem=sent.at[me, 3],
            recv_sem=arrived.at[me, 0],
            device_id=at["sibling"],
            device_id_type=MESH,
        )

    def begin():
        src = shard.at[mine, :]
        pl.when(z < LINE - 1)(lambda: pass_on(src, me, 1).start())
        pl.when(z > 0)(lambda: pass_on(src, me, 2).start())
        pass_on(src, me, 0).start()
        own_to_sibling().start()

    def relay(t, sign):
        owner = me + 2 * t * sign

        @pl.when((z - t >= 0) if sign < 0 else (z + t <= LINE - 1))
        def _():
            held = whole.at[owner, mine, :]
            pass_on(held, owner, 0).wait_recv()
            if sign < 0:
                pl.when(z < LINE - 1)(lambda: pass_on(held, owner, 1).start())
            else:
                pl.when(z > 0)(lambda: pass_on(held, owner, 2).start())
            pass_on(held, owner, 0).start()
            half_to_sibling(owner).start()

    def from_side(t, sign):
        owner = me + 1 - 2 * y + 2 * t * sign

        @pl.when((z - t >= 0) if sign < 0 else (z + t <= LINE - 1))
        def _():
            pass_on(whole.at[owner, mine, :], owner, 0).wait_recv()
            half_to_sibling(owner).start()

    def settle():
        own_to_sibling().wait_recv()
        for owner in range(2 * LINE):
            pl.when(owner != me)(lambda: half_from_sibling(owner).wait_recv())

    def drain():
        own_to_sibling().wait_send()
        src = shard.at[mine, :]
        for owner in range(2 * LINE):
            line = owner // 2
            same = owner % 2 == y

            @pl.when(same)
            def _():
                pass_on(src, owner, 0).wait_send()
                pl.when(jnp.logical_and(line <= z, z < LINE - 1))(lambda: pass_on(src, owner, 1).wait_send())
                pl.when(jnp.logical_and(line >= z, z > 0))(lambda: pass_on(src, owner, 2).wait_send())

            pl.when(owner != me)(lambda: half_to_sibling(owner).wait_send())

    relays = [functools.partial(relay, t, s) for t in range(1, LINE) for s in (-1, 1)]
    sides = [functools.partial(from_side, 0, 1)]
    sides += [functools.partial(from_side, t, s) for t in range(1, LINE) for s in (-1, 1)]
    return begin, relays, sides, settle, drain


def gather_kernel(count, *refs):
    shards, wholes, scratch = refs[:count], refs[count : 2 * count], refs[2 * count :]
    at = places()
    greet(at)
    parts = [gather_events(at, shards[g], wholes[g], scratch[2 * g : 2 * g + 2]) for g in range(count)]
    for begin, *_ in parts:
        begin()
    for _, relays, sides, *_ in parts:
        for step in relays:
            step()
    for _, relays, sides, *_ in parts:
        for step in sides:
            step()
    for part in parts:
        part[3]()
        part[4]()


def gather_all(shards, ident):
    return pl.pallas_call(
        functools.partial(gather_kernel, len(shards)),
        out_shape=[jax.ShapeDtypeStruct((2 * LINE, *s.shape), jnp.bfloat16) for s in shards],
        in_specs=[pl.BlockSpec(memory_space=pltpu.VMEM)] * len(shards),
        out_specs=[pl.BlockSpec(memory_space=pltpu.VMEM)] * len(shards),
        scratch_shapes=[x for s in shards for x in gather_scratch()],
        compiler_params=pltpu.CompilerParams(collective_id=ident, has_side_effects=True, vmem_limit_bytes=60 * 1024 * 1024),
        name="gather",
    )(*shards)


def masked_exp(scores, same):
    scores = jnp.where(same, scores, -1000000000.0)
    highest = jnp.max(scores, axis=-1, keepdims=True)
    return jnp.exp(scores - highest), highest


def cross(a, b):
    return lax.dot_general(a, b, (((1,), (1,)), ((), ())), preferred_element_type=jnp.float32)


ROWS = 256


def forward_kernel(
    pack, expand, reduce, tokens, fragment_column, fragment_row,
    attention_all, expand_all, reduce_all, queries, key_rows, value_rows, mixed, log_totals, normed, rescale,
    *scratch,
):
    rows = pack.shape[0] // 4 - SMALL // 4
    width = pack.shape[1]
    count = tokens.shape[0] // ROWS
    length = fragment_row.shape[2]
    at = places()
    greet(at)
    first = gather_events(at, pack, attention_all, scratch[0:2])
    second = gather_events(at, expand, expand_all, scratch[2:4])
    third = gather_events(at, reduce, reduce_all, scratch[4:6])
    first[0]()
    for step in first[1]:
        step()
    second[0]()
    third[0]()
    for step in first[2]:
        step()
    log_totals[...] = jnp.zeros_like(log_totals)
    first[3]()

    def weight(k):
        return attention_all[:, k * rows : (k + 1) * rows, :].reshape(-1, width)

    vectors = jnp.sum(attention_all[:, 4 * rows : 4 * rows + 16, :].astype(jnp.float32), axis=0)

    def project(i, carry):
        own = pl.ds(pl.multiple_of(i * ROWS, ROWS), ROWS)
        some = tokens[own, :]
        queries[own, :] = (
            jnp.dot(some, weight(0), preferred_element_type=jnp.float32) + vectors[0:1, :]
        ).astype(jnp.bfloat16)
        key_rows[own, :] = jnp.dot(some, weight(1), preferred_element_type=jnp.float32).astype(jnp.bfloat16)
        value_rows[own, :] = (
            jnp.dot(some, weight(2), preferred_element_type=jnp.float32) + vectors[1:2, :]
        ).astype(jnp.bfloat16)
        return carry

    lax.fori_loop(0, count, project, 0)

    pairs = width // (2 * HEAD)
    blocks = length // ROWS
    steps = count * pairs
    moves = [second[1][0:2], third[1][0:2], second[1][2:4], third[1][2:4], second[1][4:6], third[1][4:6]]
    when = [0, 4, 9, 14, 19, 23]

    def attend(i, carry):
        for due, group in zip(when, moves):

            @pl.when(i == due * steps // 24)
            def _():
                for step in group:
                    step()

        pair = lax.rem(i, pairs)
        block = i // pairs
        sequence = block // blocks
        own = pl.ds(pl.multiple_of(block * ROWS, ROWS), ROWS)
        inside = pl.ds(pl.multiple_of(lax.rem(block, blocks) * ROWS, ROWS), ROWS)
        every = pl.ds(pl.multiple_of(sequence * length, length), length)
        lanes = pl.ds(pl.multiple_of(pair * 2 * HEAD, 2 * HEAD), 2 * HEAD)
        q = queries[own, lanes].astype(jnp.float32) * (HEAD**-0.5)
        k = key_rows[every, lanes]
        v = value_rows[every, lanes]
        same = fragment_column[sequence, inside, :] == fragment_row[sequence]
        lane = lax.broadcasted_iota(jnp.int32, (ROWS, 2 * HEAD), 1)
        head_lane = lax.broadcasted_iota(jnp.int32, (ROWS, 128), 1)
        totals_now = log_totals[own, :]
        results = []
        for h in range(2):
            part = (lane >= HEAD) if h else (lane < HEAD)
            lifted, highest = masked_exp(cross(jnp.where(part, q, 0.0).astype(jnp.bfloat16), k), same)
            totals = jnp.sum(lifted, axis=-1, keepdims=True)
            out = jnp.dot(lifted.astype(jnp.bfloat16), v, preferred_element_type=jnp.float32)
            results.append(out / totals)
            totals_now = jnp.where(head_lane == 2 * pair + h, highest + jnp.log(totals), totals_now)
        mixed[own, lanes] = jnp.where(lane < HEAD, results[0], results[1]).astype(jnp.bfloat16)
        log_totals[own, :] = totals_now
        return carry

    lax.fori_loop(0, steps, attend, 0)

    def normalize(i, carry):
        own = pl.ds(pl.multiple_of(i * ROWS, ROWS), ROWS)
        total = (
            tokens[own, :].astype(jnp.float32)
            + jnp.dot(mixed[own, :], weight(3), preferred_element_type=jnp.float32)
            + vectors[2:3, :]
        )
        centered = total - jnp.mean(total, axis=-1, keepdims=True)
        scale = lax.rsqrt(jnp.mean(centered * centered, axis=-1, keepdims=True) + 1e-12)
        normed[own, :] = centered * scale
        rescale[own, :] = scale
        return carry

    lax.fori_loop(0, count, normalize, 0)
    for a, b in zip(second[2], third[2]):
        a()
        b()
    for part in (second, third):
        part[3]()
    for part in (first, second, third):
        part[4]()


def forward_all(pack, expand, reduce, tokens, segment_ids):
    low, full = jnp.bfloat16, jnp.float32
    count, width = tokens.shape
    vmem, anywhere = pl.BlockSpec(memory_space=pltpu.VMEM), pl.BlockSpec(memory_space=pl.ANY)
    shards = 2 * LINE
    flat = jax.ShapeDtypeStruct(tokens.shape, low)
    return pl.pallas_call(
        forward_kernel,
        out_shape=[
            jax.ShapeDtypeStruct((shards, *pack.shape), low),
            jax.ShapeDtypeStruct((shards, *expand.shape), low),
            jax.ShapeDtypeStruct((shards, *reduce.shape), low),
            flat, flat, flat, flat,
            jax.ShapeDtypeStruct((count, 128), full),
            jax.ShapeDtypeStruct((count, width), full),
            jax.ShapeDtypeStruct((count, 1), full),
        ],
        in_specs=[vmem, anywhere, anywhere, vmem, vmem, vmem],
        out_specs=[vmem, anywhere, anywhere] + [vmem] * 7,
        scratch_shapes=gather_scratch() * 3,
        compiler_params=pltpu.CompilerParams(
            collective_id=0, has_side_effects=True, vmem_limit_bytes=60 * 1024 * 1024
        ),
        name="forward",
    )(pack, expand, reduce, tokens, segment_ids[:, :, None], segment_ids[:, None, :])


def plain_on_device(
    tokens,
    segment_ids,
    query_weight,
    query_bias,
    key_weight,
    value_weight,
    value_bias,
    out_weight,
    out_bias,
    first_gain,
    first_shift,
    expand_weight,
    expand_bias,
    reduce_weight,
    reduce_bias,
    second_gain,
    second_shift,
    cotangent,
):
    seq_count, seq_length = segment_ids.shape
    shaped = (seq_count, seq_length, HEADS, HEAD)
    rows, width = query_weight.shape
    small = (query_bias, value_bias, out_bias, first_gain, first_shift, reduce_bias, second_gain, second_shift)
    small_pack = jnp.concatenate([v[None, :] for v in small] + [expand_bias.reshape(-1, rows)], axis=0)
    gathered_small = lax.all_gather(small_pack, "fsdp", axis=1, tiled=True)
    groups = gathered_small.shape[1] // rows
    vectors = [gathered_small[k] for k in range(8)]
    expand_bias_all = (
        gathered_small[8:].reshape(-1, groups, rows).transpose(1, 0, 2).reshape(groups * expand_bias.shape[0])
    )
    query_bias_all, value_bias_all, out_bias_all, gain1, shift1, reduce_bias_all, gain2, shift2 = vectors
    attention_pack = jnp.stack([query_weight, key_weight, value_weight, out_weight])
    attention_all = lax.all_gather(attention_pack, "fsdp", axis=1, tiled=True)
    expand_all = lax.all_gather(expand_weight, "fsdp", axis=0, tiled=True)
    reduce_all = lax.all_gather(reduce_weight, "fsdp", axis=0, tiled=True)
    wq, wk, wv, wo = attention_all[0], attention_all[1], attention_all[2], attention_all[3]

    queries = linear(tokens, wq, query_bias_all).astype(jnp.bfloat16).reshape(shaped)
    key_rows = jnp.dot(tokens, wk, preferred_element_type=jnp.float32).astype(jnp.bfloat16).reshape(shaped)
    value_rows = linear(tokens, wv, value_bias_all).astype(jnp.bfloat16).reshape(shaped)
    mixed, log_totals = lax.map(attend_forward, (queries, key_rows, value_rows, segment_ids))
    mixed = mixed.reshape(tokens.shape)
    first_sum = tokens.astype(jnp.float32) + linear(mixed, wo, out_bias_all)
    hidden, first_normed, first_rescale = layer_norm(first_sum, gain1, shift1)
    hidden_low = hidden.astype(jnp.bfloat16)
    inner = linear(hidden_low, expand_all, expand_bias_all)
    active = jax.nn.gelu(inner, approximate=False).astype(jnp.bfloat16)
    second_sum = hidden + linear(active, reduce_all, reduce_bias_all)
    output, second_normed, second_rescale = layer_norm(second_sum, gain2, shift2)
    second_grad, grad_second_gain, grad_second_shift = norm_back(
        cotangent.astype(jnp.float32), second_normed, second_rescale, gain2
    )
    branch_grad = second_grad.astype(jnp.bfloat16)
    grad_reduce = weight_grad(active, branch_grad)
    grad_reduce_bias = bias_grad(branch_grad)
    inner_grad = (back_rows(branch_grad, reduce_all) * gelu_slope(inner)).astype(jnp.bfloat16)
    grad_expand = weight_grad(hidden_low, inner_grad)
    grad_expand_bias = bias_grad(inner_grad)
    hidden_grad = second_grad + back_rows(inner_grad, expand_all)
    low = jnp.bfloat16
    scattered_expand = lax.psum_scatter(grad_expand.astype(low), "fsdp", scatter_dimension=0, tiled=True)
    scattered_reduce = lax.psum_scatter(grad_reduce.astype(low), "fsdp", scatter_dimension=0, tiled=True)
    first_grad, grad_first_gain, grad_first_shift = norm_back(
        hidden_grad, first_normed, first_rescale, gain1
    )
    out_grad = first_grad.astype(jnp.bfloat16)
    grad_out = weight_grad(mixed, out_grad)
    grad_out_bias = bias_grad(out_grad)
    mixed_grad = back_rows(out_grad, wo).astype(jnp.bfloat16).reshape(shaped)
    query_grad, key_grad, value_grad = lax.map(
        attend_backward, (queries, key_rows, value_rows, segment_ids, mixed_grad, log_totals)
    )
    query_grad = query_grad.reshape(tokens.shape)
    key_grad = key_grad.reshape(tokens.shape)
    value_grad = value_grad.reshape(tokens.shape)
    grad_query = weight_grad(tokens, query_grad)
    grad_query_bias = bias_grad(query_grad)
    grad_key = weight_grad(tokens, key_grad)
    grad_value = weight_grad(tokens, value_grad)
    grad_value_bias = bias_grad(value_grad)
    input_grad = first_grad + back_rows(query_grad, wq) + back_rows(key_grad, wk) + back_rows(value_grad, wv)
    small_grads = (
        grad_query_bias, grad_value_bias, grad_out_bias, grad_first_gain, grad_first_shift,
        grad_reduce_bias, grad_second_gain, grad_second_shift,
    )
    small_sum = jnp.concatenate(
        [v[None, :] for v in small_grads]
        + [grad_expand_bias.reshape(groups, -1, rows).transpose(1, 0, 2).reshape(-1, groups * rows)],
        axis=0,
    )
    small_sum = lax.psum(small_sum, ("dp", "fsdp"))
    at = lax.axis_index("fsdp") * rows
    small_own = lax.dynamic_slice_in_dim(small_sum, at, rows, axis=1)
    attention_grads = jnp.concatenate([grad_query, grad_key, grad_value, grad_out], axis=1).astype(low)
    attention_own = lax.psum_scatter(attention_grads, "fsdp", scatter_dimension=0, tiled=True)
    attention_own = lax.psum(attention_own, "dp").astype(jnp.float32)
    attention_own = [attention_own[:, k * width : (k + 1) * width] for k in range(4)]
    expand_own = lax.psum(scattered_expand, "dp").astype(jnp.float32)
    reduce_own = lax.psum(scattered_reduce, "dp").astype(jnp.float32)
    return (
        output.astype(jnp.bfloat16),
        input_grad,
        attention_own[0],
        small_own[0],
        attention_own[1],
        attention_own[2],
        small_own[1],
        attention_own[3],
        small_own[2],
        small_own[3],
        small_own[4],
        expand_own,
        small_own[8:].reshape(-1),
        reduce_own,
        small_own[5],
        small_own[6],
        small_own[7],
    )


def on_device(
    tokens,
    segment_ids,
    query_weight,
    query_bias,
    key_weight,
    value_weight,
    value_bias,
    out_weight,
    out_bias,
    first_gain,
    first_shift,
    expand_weight,
    expand_bias,
    reduce_weight,
    reduce_bias,
    second_gain,
    second_shift,
    cotangent,
):
    seq_count, seq_length = segment_ids.shape
    shaped = (seq_count, seq_length, HEADS, HEAD)
    rows, width = query_weight.shape
    low = jnp.bfloat16
    me = lax.axis_index("fsdp")
    shards = 2 * LINE
    vectors = jnp.stack(
        [query_bias, value_bias, out_bias, first_gain, first_shift, reduce_bias, second_gain, second_shift]
    )
    count = expand_bias.shape[0]
    per_row = width // count
    small = lax.dynamic_update_slice(jnp.zeros((SMALL, width), low), vectors, (0, me * rows))
    small = lax.dynamic_update_slice(small, expand_bias[None, :], (8 + me // per_row, lax.rem(me, per_row) * count))
    pack = jnp.concatenate([query_weight, key_weight, value_weight, out_weight, small], axis=0)
    (
        attention_all, expand_all, reduce_all, queries, key_rows, value_rows, mixed, log_totals, first_normed, first_rescale,
    ) = forward_all(pack, expand_weight, reduce_weight, tokens, segment_ids)
    wq, wk, wv, wo = [attention_all[:, k * rows : (k + 1) * rows].reshape(width, width) for k in range(4)]
    small_all = jnp.sum(attention_all[:, 4 * rows :].astype(jnp.float32), axis=0)
    query_bias_all, value_bias_all, out_bias_all, gain1, shift1, reduce_bias_all, gain2, shift2 = [
        small_all[k] for k in range(8)
    ]
    expand_bias_all = small_all[8 : 8 + shards // per_row].reshape(-1)
    expand_all = expand_all.reshape(width, -1)
    reduce_all = reduce_all.reshape(-1, width)

    queries, key_rows, value_rows = [x.reshape(shaped) for x in (queries, key_rows, value_rows)]
    log_totals = log_totals.reshape(seq_count, seq_length, -1)[:, :, :HEADS].transpose(0, 2, 1)[..., None]
    hidden = first_normed * gain1 + shift1
    hidden_low = hidden.astype(jnp.bfloat16)
    inner = linear(hidden_low, expand_all, expand_bias_all)
    active = jax.nn.gelu(inner, approximate=False).astype(jnp.bfloat16)
    second_sum = hidden + linear(active, reduce_all, reduce_bias_all)
    output, second_normed, second_rescale = layer_norm(second_sum, gain2, shift2)
    second_grad, grad_second_gain, grad_second_shift = norm_back(
        cotangent.astype(jnp.float32), second_normed, second_rescale, gain2
    )
    branch_grad = second_grad.astype(jnp.bfloat16)
    grad_reduce = weight_grad(active, branch_grad)
    grad_reduce_bias = bias_grad(branch_grad)
    inner_grad = (back_rows(branch_grad, reduce_all) * gelu_slope(inner)).astype(jnp.bfloat16)
    grad_expand = weight_grad(hidden_low, inner_grad)
    grad_expand_bias = bias_grad(inner_grad)
    hidden_grad = second_grad + back_rows(inner_grad, expand_all)
    expand_own, reduce_own = scatter_all(
        [
            grad_expand.astype(low).reshape(LINE, 2, rows, -1),
            grad_reduce.astype(low).reshape(LINE, 2, -1, width),
        ],
        2,
    )
    first_grad, grad_first_gain, grad_first_shift = norm_back(
        hidden_grad, first_normed, first_rescale, gain1
    )
    out_grad = first_grad.astype(jnp.bfloat16)
    grad_out = weight_grad(mixed, out_grad)
    grad_out_bias = bias_grad(out_grad)
    mixed_grad = back_rows(out_grad, wo).astype(jnp.bfloat16).reshape(shaped)
    query_grad, key_grad, value_grad = lax.map(
        attend_backward, (queries, key_rows, value_rows, segment_ids, mixed_grad, log_totals)
    )
    query_grad = query_grad.reshape(tokens.shape)
    key_grad = key_grad.reshape(tokens.shape)
    value_grad = value_grad.reshape(tokens.shape)
    grad_query = weight_grad(tokens, query_grad)
    grad_query_bias = bias_grad(query_grad)
    grad_key = weight_grad(tokens, key_grad)
    grad_value = weight_grad(tokens, value_grad)
    grad_value_bias = bias_grad(value_grad)
    input_grad = first_grad + back_rows(query_grad, wq) + back_rows(key_grad, wk) + back_rows(value_grad, wv)
    small_grads = (
        grad_query_bias, grad_value_bias, grad_out_bias, grad_first_gain, grad_first_shift,
        grad_reduce_bias, grad_second_gain, grad_second_shift,
    )
    small_grads = jnp.stack(small_grads).reshape(8, shards, rows).transpose(1, 0, 2)
    small_grads = jnp.concatenate([small_grads, grad_expand_bias.reshape(shards, -1, rows)], axis=1)
    small_grads = jnp.pad(
        small_grads.astype(low), ((0, 0), (0, SMALL - small_grads.shape[1]), (0, width - rows))
    )
    attention_grads = jnp.concatenate(
        [g.astype(low).reshape(shards, rows, width) for g in (grad_query, grad_key, grad_value, grad_out)]
        + [small_grads],
        axis=1,
    )
    (attention_own,) = scatter_all([attention_grads.reshape(LINE, 2, -1, width)], 3)
    attention_own = attention_own.astype(jnp.float32)
    small_own = attention_own[4 * rows :, :rows]
    attention_own = [attention_own[k * rows : (k + 1) * rows] for k in range(4)]
    return (
        output.astype(low),
        input_grad,
        attention_own[0],
        small_own[0],
        attention_own[1],
        attention_own[2],
        small_own[1],
        attention_own[3],
        small_own[2],
        small_own[3],
        small_own[4],
        expand_own.astype(jnp.float32),
        small_own[8 : 8 + count // rows].reshape(-1),
        reduce_own.astype(jnp.float32),
        small_own[5],
        small_own[6],
        small_own[7],
    )


def solution(mesh):
    fits = mesh.shape["fsdp"] == 2 * LINE and mesh.shape["dp"] == 4
    body = on_device if fits else plain_on_device
    in_specs = (
        P(("dp", "fsdp"), None),
        P(("dp", "fsdp"), None),
        P("fsdp", None),
        P("fsdp"),
        P("fsdp", None),
        P("fsdp", None),
        P("fsdp"),
        P("fsdp", None),
        P("fsdp"),
        P("fsdp"),
        P("fsdp"),
        P("fsdp", None),
        P("fsdp"),
        P("fsdp", None),
        P("fsdp"),
        P("fsdp"),
        P("fsdp"),
        P(("dp", "fsdp"), None),
    )
    out_specs = (
        P(("dp", "fsdp"), None),
        P(("dp", "fsdp"), None),
        P("fsdp", None),
        P("fsdp"),
        P("fsdp", None),
        P("fsdp", None),
        P("fsdp"),
        P("fsdp", None),
        P("fsdp"),
        P("fsdp"),
        P("fsdp"),
        P("fsdp", None),
        P("fsdp"),
        P("fsdp", None),
        P("fsdp"),
        P("fsdp"),
        P("fsdp"),
    )
    return jax.shard_map(
        body, mesh=mesh, in_specs=in_specs, out_specs=out_specs, check_vma=False
    )
```

```python
import functools

import jax
import jax.numpy as jnp
from jax import lax
from jax.experimental import pallas as pl
from jax.experimental.pallas import tpu as pltpu
from jax.sharding import PartitionSpec as P

HEADS = 12
HEAD = 64
SMALL = 32


def layer_norm(rows, gain, shift):
    average = jnp.mean(rows, axis=-1, keepdims=True)
    centered = rows - average
    rescale = lax.rsqrt(jnp.mean(centered * centered, axis=-1, keepdims=True) + 1e-12)
    normed = centered * rescale
    return (normed * gain.astype(jnp.float32) + shift.astype(jnp.float32), normed, rescale)


def norm_back(gradient, normed, rescale, gain):
    scaled = gradient * gain.astype(jnp.float32)
    inner_mean = jnp.mean(scaled * normed, axis=-1, keepdims=True)
    rows_grad = rescale * (scaled - jnp.mean(scaled, axis=-1, keepdims=True) - normed * inner_mean)
    return (rows_grad, jnp.sum(gradient * normed, axis=0), jnp.sum(gradient, axis=0))


def linear(rows, weight, bias):
    return jnp.dot(rows, weight, preferred_element_type=jnp.float32) + bias.astype(jnp.float32)


def weight_grad(rows, gradient):
    return jnp.einsum("ti,to->io", rows, gradient, preferred_element_type=jnp.float32)


def bias_grad(gradient):
    return jnp.sum(gradient.astype(jnp.float32), axis=0)


def back_rows(gradient, weight):
    return jnp.einsum("to,io->ti", gradient, weight, preferred_element_type=jnp.float32)


def gelu_slope(inner):
    normal_cdf = 0.5 * (1.0 + lax.erf(inner * 0.7071067811865476))
    density = jnp.exp(-0.5 * inner * inner) * 0.3989422804014327
    return normal_cdf + inner * density


def masked_scores(queries, key_rows, fragment):
    scaling = queries.shape[-1] ** (-0.5)
    scores = (
        jnp.einsum("qhd,khd->hqk", queries, key_rows, preferred_element_type=jnp.float32) * scaling
    )
    same_fragment = fragment[:, None] == fragment[None, :]
    return jnp.where(same_fragment[None, :, :], scores, -1000000000.0)


def attend_forward(bundle):
    queries, key_rows, value_rows, fragment = bundle
    scores = masked_scores(queries, key_rows, fragment)
    highest = jnp.max(scores, axis=-1, keepdims=True)
    lifted = jnp.exp(scores - highest)
    totals = jnp.sum(lifted, axis=-1, keepdims=True)
    weights = (lifted / totals).astype(jnp.bfloat16)
    mixed = jnp.einsum("hqk,khd->qhd", weights, value_rows, preferred_element_type=jnp.float32)
    return (mixed.astype(jnp.bfloat16), highest + jnp.log(totals))


def attend_backward(bundle):
    queries, key_rows, value_rows, fragment, mixed_grad, log_totals = bundle
    scaling = queries.shape[-1] ** (-0.5)
    weights = jnp.exp(masked_scores(queries, key_rows, fragment) - log_totals)
    value_grad = jnp.einsum(
        "hqk,qhd->khd", weights.astype(jnp.bfloat16), mixed_grad, preferred_element_type=jnp.float32
    )
    prob_grad = jnp.einsum(
        "qhd,khd->hqk", mixed_grad, value_rows, preferred_element_type=jnp.float32
    )
    score_grad = (
        weights * (prob_grad - jnp.sum(prob_grad * weights, axis=-1, keepdims=True))
    ).astype(jnp.bfloat16)
    query_grad = (
        jnp.einsum("hqk,khd->qhd", score_grad, key_rows, preferred_element_type=jnp.float32)
        * scaling
    )
    key_grad = (
        jnp.einsum("hqk,qhd->khd", score_grad, queries, preferred_element_type=jnp.float32)
        * scaling
    )
    return (
        query_grad.astype(jnp.bfloat16),
        key_grad.astype(jnp.bfloat16),
        value_grad.astype(jnp.bfloat16),
    )


MESH = pl.DeviceIdType.MESH
LINE = 4
ORDER = (3, 0, 2, 1)


def places():
    dp, fs = lax.axis_index("dp"), lax.axis_index("fsdp")
    core, y, z = lax.rem(dp, 2), lax.rem(fs, 2), fs // 2
    return dict(
        core=core, y=y, z=z, fs=fs,
        sibling=(dp + 1 - 2 * core, fs),
        across=(lax.rem(dp + 2, 4), fs),
        side=(dp, fs + 1 - 2 * y),
        up=(dp, fs + 2),
        down=(dp, fs - 2),
    )


def greet(at):
    barrier = pltpu.get_barrier_semaphore()

    def hello(who):
        pl.semaphore_signal(barrier, inc=1, device_id=who, device_id_type=MESH)

    for name in ("sibling", "across", "side"):
        hello(at[name])
    pl.when(at["z"] < LINE - 1)(lambda: hello(at["up"]))
    pl.when(at["z"] > 0)(lambda: hello(at["down"]))
    end = jnp.logical_or(at["z"] == 0, at["z"] == LINE - 1)
    pl.when(end)(lambda: pl.semaphore_wait(barrier, 4))
    pl.when(jnp.logical_not(end))(lambda: pl.semaphore_wait(barrier, 5))


def add_rows(target, *sources):
    rows = target.shape[0]

    def block(k, carry):
        at = pl.ds(pl.multiple_of(k * 16, 16), 16)
        total = sources[0][at, :].astype(jnp.float32)
        for source in sources[1:]:
            total = total + source[at, :].astype(jnp.float32)
        target[at, :] = total.astype(jnp.bfloat16)
        return carry

    lax.fori_loop(0, rows // 16, block, 0)


def scatter_scratch(rows, columns):
    half = rows // 2
    low = jnp.bfloat16
    return [
        pltpu.VMEM((2, LINE, half, columns), low),
        pltpu.VMEM((2, LINE, half, columns), low),
        pltpu.VMEM((LINE, half, columns), low),
        pltpu.VMEM((2, LINE, half, columns), low),
        pltpu.VMEM((half, columns), low),
        pltpu.VMEM((2, half, columns), low),
        pltpu.SemaphoreType.DMA((2,)),
        pltpu.SemaphoreType.DMA((2, 2)),
        pltpu.SemaphoreType.DMA((2, LINE)),
        pltpu.SemaphoreType.DMA((2, 2, LINE)),
        pltpu.SemaphoreType.DMA((2, 2)),
    ]


SCRATCHES = 11


def scatter_events(at, source, out, scratch):
    own, sib, side, line, across, result, load_sem, sib_sem, side_sem, line_sem, last_sem = scratch
    half = own.shape[2]
    core, y, z = at["core"], at["y"], at["z"]
    mine = pl.ds(pl.multiple_of(core * half, 16), half)
    other = pl.ds(pl.multiple_of((1 - core) * half, 16), half)
    column = (1 - y, y)

    def load(k):
        return pltpu.make_async_copy(source.at[:, column[k], mine, :], own.at[k], load_sem.at[k])

    def remote(src, dst, send, recv, who):
        return pltpu.make_async_remote_copy(
            src_ref=src, dst_ref=dst, send_sem=send, recv_sem=recv, device_id=at[who], device_id_type=MESH
        )

    def to_sibling(k):
        return remote(source.at[:, column[k], other, :], sib.at[k], sib_sem.at[0, k], sib_sem.at[1, k], "sibling")

    def to_side(k):
        return remote(own.at[0, k], side.at[k], side_sem.at[0, k], side_sem.at[1, k], "side")

    def to_line(way, k):
        return remote(
            own.at[1, k], line.at[way, k], line_sem.at[0, way, k], line_sem.at[1, way, k], ("up", "down")[way]
        )

    def to_across():
        return remote(own.at[1, z], across, last_sem.at[0, 0], last_sem.at[1, 0], "across")

    def to_last():
        return remote(result.at[core], result.at[core], last_sem.at[0, 1], last_sem.at[1, 1], "sibling")

    def begin():
        for k in range(2):
            to_sibling(k).start()
            load(k).start()

    def first():
        load(0).wait()
        to_sibling(0).wait_recv()
        for k in ORDER:
            add_rows(own.at[0, k], own.at[0, k], sib.at[0, k])
            to_side(k).start()
        load(1).wait()
        to_sibling(1).wait_recv()
        for k in ORDER:
            add_rows(own.at[1, k], own.at[1, k], sib.at[1, k])

    def chain(k):
        to_side(k).wait_recv()

        def pass_on(way, inner):
            @pl.when(inner)
            def _():
                to_line(way, k).wait_recv()
                add_rows(own.at[1, k], own.at[1, k], side.at[k], line.at[way, k])

            @pl.when(jnp.logical_not(inner))
            def _():
                add_rows(own.at[1, k], own.at[1, k], side.at[k])

            to_line(way, k).start()

        pl.when(k > z)(lambda: pass_on(0, z > 0))
        pl.when(k < z)(lambda: pass_on(1, z < LINE - 1))
        pl.when(k == z)(lambda: add_rows(own.at[1, k], own.at[1, k], side.at[k]))

    def gather_line():
        for k in range(LINE):

            @pl.when(k == z)
            def _():
                parts = []
                if k > 0:
                    to_line(0, k).wait_recv()
                    parts.append(line.at[0, k])
                if k < LINE - 1:
                    to_line(1, k).wait_recv()
                    parts.append(line.at[1, k])
                add_rows(own.at[1, k], own.at[1, k], *parts)

        to_across().start()

    def finish():
        to_across().wait_recv()
        add_rows(result.at[core], own.at[1, z], across)
        to_last().start()

    def drain():
        to_last().wait_recv()
        out[0:half, :] = result[0]
        out[half : 2 * half, :] = result[1]
        to_last().wait_send()
        to_across().wait_send()
        for k in range(2):
            to_sibling(k).wait_send()
        for k in range(LINE):
            to_side(k).wait_send()
            pl.when(k > z)(lambda: to_line(0, k).wait_send())
            pl.when(k < z)(lambda: to_line(1, k).wait_send())

    chains = [functools.partial(chain, k) for k in ORDER]
    return begin, first, chains, gather_line, finish, drain


def scatter_kernel(count, *refs):
    sources, outs, scratch = refs[:count], refs[count : 2 * count], refs[2 * count :]
    at = places()
    greet(at)
    parts = [
        scatter_events(at, sources[g], outs[g], scratch[g * SCRATCHES : (g + 1) * SCRATCHES]) for g in range(count)
    ]
    for begin, *_ in parts:
        begin()
    for _, first, *_ in parts:
        first()
    for _, _, chains, *_ in parts:
        for step in chains:
            step()
    for part in parts:
        part[3]()
    for part in parts:
        part[4]()
    for part in parts:
        part[5]()


def scatter_all(sources, ident):
    shapes = [s.shape[2:] for s in sources]
    return pl.pallas_call(
        functools.partial(scatter_kernel, len(sources)),
        out_shape=[jax.ShapeDtypeStruct(s, jnp.bfloat16) for s in shapes],
        in_specs=[pl.BlockSpec(memory_space=pl.ANY)] * len(sources),
        out_specs=[pl.BlockSpec(memory_space=pltpu.VMEM)] * len(sources),
        scratch_shapes=[x for s in shapes for x in scatter_scratch(*s)],
        compiler_params=pltpu.CompilerParams(
            collective_id=ident, has_side_effects=True, vmem_limit_bytes=60 * 1024 * 1024
        ),
        name="scatter_sum",
    )(*sources)


def gather_scratch():
    return [pltpu.SemaphoreType.DMA((2 * LINE, 2)), pltpu.SemaphoreType.DMA((2 * LINE, 4))]


def gather_events(at, shard, whole, scratch):
    arrived, sent = scratch
    half = shard.shape[0] // 2
    core, y, z, me = at["core"], at["y"], at["z"], at["fs"]
    mine = pl.ds(pl.multiple_of(core * half, 16), half)
    ways = ("side", "up", "down")

    def pass_on(src, owner, way):
        return pltpu.make_async_remote_copy(
            src_ref=src,
            dst_ref=whole.at[owner, mine, :],
            send_sem=sent.at[owner, way],
            recv_sem=arrived.at[owner, core],
            device_id=at[ways[way]],
            device_id_type=MESH,
        )

    def half_to_sibling(owner):
        return pltpu.make_async_remote_copy(
            src_ref=whole.at[owner, mine, :],
            dst_ref=whole.at[owner, mine, :],
            send_sem=sent.at[owner, 3],
            recv_sem=arrived.at[owner, core],
            device_id=at["sibling"],
            device_id_type=MESH,
        )

    def half_from_sibling(owner):
        theirs = pl.ds(pl.multiple_of((1 - core) * half, 16), half)
        return pltpu.make_async_remote_copy(
            src_ref=whole.at[owner, theirs, :],
            dst_ref=whole.at[owner, theirs, :],
            send_sem=sent.at[owner, 3],
            recv_sem=arrived.at[owner, 1 - core],
            device_id=at["sibling"],
            device_id_type=MESH,
        )

    def own_to_sibling():
        return pltpu.make_async_remote_copy(
            src_ref=shard,
            dst_ref=whole.at[me],
            send_sem=sent.at[me, 3],
            recv_sem=arrived.at[me, 0],
            device_id=at["sibling"],
            device_id_type=MESH,
        )

    def begin():
        src = shard.at[mine, :]
        pl.when(z < LINE - 1)(lambda: pass_on(src, me, 1).start())
        pl.when(z > 0)(lambda: pass_on(src, me, 2).start())
        pass_on(src, me, 0).start()
        own_to_sibling().start()

    def relay(t, sign):
        owner = me + 2 * t * sign

        @pl.when((z - t >= 0) if sign < 0 else (z + t <= LINE - 1))
        def _():
            held = whole.at[owner, mine, :]
            pass_on(held, owner, 0).wait_recv()
            if sign < 0:
                pl.when(z < LINE - 1)(lambda: pass_on(held, owner, 1).start())
            else:
                pl.when(z > 0)(lambda: pass_on(held, owner, 2).start())
            pass_on(held, owner, 0).start()
            half_to_sibling(owner).start()

    def from_side(t, sign):
        owner = me + 1 - 2 * y + 2 * t * sign

        @pl.when((z - t >= 0) if sign < 0 else (z + t <= LINE - 1))
        def _():
            pass_on(whole.at[owner, mine, :], owner, 0).wait_recv()
            half_to_sibling(owner).start()

    def settle():
        own_to_sibling().wait_recv()
        for owner in range(2 * LINE):
            pl.when(owner != me)(lambda: half_from_sibling(owner).wait_recv())

    def drain():
        own_to_sibling().wait_send()
        src = shard.at[mine, :]
        for owner in range(2 * LINE):
            line = owner // 2
            same = owner % 2 == y

            @pl.when(same)
            def _():
                pass_on(src, owner, 0).wait_send()
                pl.when(jnp.logical_and(line <= z, z < LINE - 1))(lambda: pass_on(src, owner, 1).wait_send())
                pl.when(jnp.logical_and(line >= z, z > 0))(lambda: pass_on(src, owner, 2).wait_send())

            pl.when(owner != me)(lambda: half_to_sibling(owner).wait_send())

    relays = [functools.partial(relay, t, s) for t in range(1, LINE) for s in (-1, 1)]
    sides = [functools.partial(from_side, 0, 1)]
    sides += [functools.partial(from_side, t, s) for t in range(1, LINE) for s in (-1, 1)]
    return begin, relays, sides, settle, drain


def gather_kernel(count, *refs):
    shards, wholes, scratch = refs[:count], refs[count : 2 * count], refs[2 * count :]
    at = places()
    greet(at)
    parts = [gather_events(at, shards[g], wholes[g], scratch[2 * g : 2 * g + 2]) for g in range(count)]
    for begin, *_ in parts:
        begin()
    for _, relays, sides, *_ in parts:
        for step in relays:
            step()
    for _, relays, sides, *_ in parts:
        for step in sides:
            step()
    for part in parts:
        part[3]()
        part[4]()


def gather_all(shards, ident):
    return pl.pallas_call(
        functools.partial(gather_kernel, len(shards)),
        out_shape=[jax.ShapeDtypeStruct((2 * LINE, *s.shape), jnp.bfloat16) for s in shards],
        in_specs=[pl.BlockSpec(memory_space=pltpu.VMEM)] * len(shards),
        out_specs=[pl.BlockSpec(memory_space=pltpu.VMEM)] * len(shards),
        scratch_shapes=[x for s in shards for x in gather_scratch()],
        compiler_params=pltpu.CompilerParams(collective_id=ident, has_side_effects=True, vmem_limit_bytes=60 * 1024 * 1024),
        name="gather",
    )(*shards)


def masked_exp(scores, same):
    scores = jnp.where(same, scores, -1000000000.0)
    highest = jnp.max(scores, axis=-1, keepdims=True)
    return jnp.exp(scores - highest), highest


def cross(a, b):
    return lax.dot_general(a, b, (((1,), (1,)), ((), ())), preferred_element_type=jnp.float32)


ROWS = 256


def forward_kernel(
    pack, expand, reduce, tokens, fragment_column, fragment_row,
    attention_all, expand_all, reduce_all, queries, key_rows, value_rows, mixed, log_totals, normed, rescale,
    *scratch,
):
    rows = pack.shape[0] // 4 - SMALL // 4
    width = pack.shape[1]
    count = tokens.shape[0] // ROWS
    length = fragment_row.shape[2]
    at = places()
    greet(at)
    first = gather_events(at, pack, attention_all, scratch[0:2])
    second = gather_events(at, expand, expand_all, scratch[2:4])
    third = gather_events(at, reduce, reduce_all, scratch[4:6])
    first[0]()
    for step in first[1]:
        step()
    second[0]()
    third[0]()
    for step in first[2]:
        step()
    log_totals[...] = jnp.zeros_like(log_totals)
    first[3]()

    def weight(k):
        return attention_all[:, k * rows : (k + 1) * rows, :].reshape(-1, width)

    vectors = jnp.sum(attention_all[:, 4 * rows : 4 * rows + 16, :].astype(jnp.float32), axis=0)

    def project(i, carry):
        own = pl.ds(pl.multiple_of(i * ROWS, ROWS), ROWS)
        some = tokens[own, :]
        queries[own, :] = (
            jnp.dot(some, weight(0), preferred_element_type=jnp.float32) + vectors[0:1, :]
        ).astype(jnp.bfloat16)
        key_rows[own, :] = jnp.dot(some, weight(1), preferred_element_type=jnp.float32).astype(jnp.bfloat16)
        value_rows[own, :] = (
            jnp.dot(some, weight(2), preferred_element_type=jnp.float32) + vectors[1:2, :]
        ).astype(jnp.bfloat16)
        return carry

    lax.fori_loop(0, count, project, 0)

    pairs = width // (2 * HEAD)
    blocks = length // ROWS
    steps = count * pairs
    moves = [second[1][0:2], third[1][0:2], second[1][2:4], third[1][2:4], second[1][4:6], third[1][4:6]]
    when = [0, 4, 9, 14, 19, 23]

    def attend(i, carry):
        for due, group in zip(when, moves):

            @pl.when(i == due * steps // 24)
            def _():
                for step in group:
                    step()

        pair = lax.rem(i, pairs)
        block = i // pairs
        sequence = block // blocks
        own = pl.ds(pl.multiple_of(block * ROWS, ROWS), ROWS)
        inside = pl.ds(pl.multiple_of(lax.rem(block, blocks) * ROWS, ROWS), ROWS)
        every = pl.ds(pl.multiple_of(sequence * length, length), length)
        lanes = pl.ds(pl.multiple_of(pair * 2 * HEAD, 2 * HEAD), 2 * HEAD)
        q = queries[own, lanes].astype(jnp.float32) * (HEAD**-0.5)
        k = key_rows[every, lanes]
        v = value_rows[every, lanes]
        same = fragment_column[sequence, inside, :] == fragment_row[sequence]
        lane = lax.broadcasted_iota(jnp.int32, (ROWS, 2 * HEAD), 1)
        head_lane = lax.broadcasted_iota(jnp.int32, (ROWS, 128), 1)
        totals_now = log_totals[own, :]
        results = []
        for h in range(2):
            part = (lane >= HEAD) if h else (lane < HEAD)
            lifted, highest = masked_exp(cross(jnp.where(part, q, 0.0).astype(jnp.bfloat16), k), same)
            totals = jnp.sum(lifted, axis=-1, keepdims=True)
            out = jnp.dot(lifted.astype(jnp.bfloat16), v, preferred_element_type=jnp.float32)
            results.append(out / totals)
            totals_now = jnp.where(head_lane == 2 * pair + h, highest + jnp.log(totals), totals_now)
        mixed[own, lanes] = jnp.where(lane < HEAD, results[0], results[1]).astype(jnp.bfloat16)
        log_totals[own, :] = totals_now
        return carry

    lax.fori_loop(0, steps, attend, 0)

    def normalize(i, carry):
        own = pl.ds(pl.multiple_of(i * ROWS, ROWS), ROWS)
        total = (
            tokens[own, :].astype(jnp.float32)
            + jnp.dot(mixed[own, :], weight(3), preferred_element_type=jnp.float32)
            + vectors[2:3, :]
        )
        centered = total - jnp.mean(total, axis=-1, keepdims=True)
        scale = lax.rsqrt(jnp.mean(centered * centered, axis=-1, keepdims=True) + 1e-12)
        normed[own, :] = centered * scale
        rescale[own, :] = scale
        return carry

    lax.fori_loop(0, count, normalize, 0)
    for a, b in zip(second[2], third[2]):
        a()
        b()
    for part in (second, third):
        part[3]()
    for part in (first, second, third):
        part[4]()


def forward_all(pack, expand, reduce, tokens, segment_ids):
    low, full = jnp.bfloat16, jnp.float32
    count, width = tokens.shape
    vmem, anywhere = pl.BlockSpec(memory_space=pltpu.VMEM), pl.BlockSpec(memory_space=pl.ANY)
    shards = 2 * LINE
    flat = jax.ShapeDtypeStruct(tokens.shape, low)
    return pl.pallas_call(
        forward_kernel,
        out_shape=[
            jax.ShapeDtypeStruct((shards, *pack.shape), low),
            jax.ShapeDtypeStruct((shards, *expand.shape), low),
            jax.ShapeDtypeStruct((shards, *reduce.shape), low),
            flat, flat, flat, flat,
            jax.ShapeDtypeStruct((count, 128), full),
            jax.ShapeDtypeStruct((count, width), full),
            jax.ShapeDtypeStruct((count, 1), full),
        ],
        in_specs=[vmem, anywhere, anywhere, vmem, vmem, vmem],
        out_specs=[vmem, anywhere, anywhere] + [vmem] * 7,
        scratch_shapes=gather_scratch() * 3,
        compiler_params=pltpu.CompilerParams(
            collective_id=0, has_side_effects=True, vmem_limit_bytes=60 * 1024 * 1024
        ),
        name="forward",
    )(pack, expand, reduce, tokens, segment_ids[:, :, None], segment_ids[:, None, :])


def inward(a, b):
    return lax.dot_general(a, b, (((0,), (0,)), ((), ())), preferred_element_type=jnp.float32)


def backward_kernel(
    grad_expand, grad_reduce, out_grad, out_weight, queries, key_rows, value_rows, log_totals,
    fragment_column, fragment_row,
    expand_own, reduce_own, query_grad, key_grad, value_grad,
    mixed_grad, *scratch,
):
    width = out_grad.shape[1]
    count = out_grad.shape[0] // ROWS
    length = fragment_row.shape[2]
    blocks = length // ROWS
    at = places()
    greet(at)
    one = scatter_events(at, grad_expand, expand_own, scratch[:SCRATCHES])
    two = scatter_events(at, grad_reduce, reduce_own, scratch[SCRATCHES:])
    one[0]()
    two[0]()

    def spread(i, carry):
        own = pl.ds(pl.multiple_of(i * ROWS, ROWS), ROWS)
        mixed_grad[own, :] = cross(out_grad[own, :], out_weight[...]).astype(jnp.bfloat16)
        return carry

    one[1]()
    two[1]()
    lax.fori_loop(0, count, spread, 0)

    pairs = width // (2 * HEAD)
    steps = fragment_row.shape[0] * pairs
    moves = [(5, one[2][0]), (7, one[2][1]), (9, one[2][2]), (11, one[2][3])]

    def attend(i, carry):
        for due, step in moves:
            pl.when(i == due * steps // 12)(step)

        pair = lax.rem(i, pairs)
        sequence = i // pairs
        every = pl.ds(pl.multiple_of(sequence * length, length), length)
        lanes = pl.ds(pl.multiple_of(pair * 2 * HEAD, 2 * HEAD), 2 * HEAD)
        k = key_rows[every, lanes]
        v = value_rows[every, lanes]
        lane = lax.broadcasted_iota(jnp.int32, (ROWS, 2 * HEAD), 1)
        head_lane = lax.broadcasted_iota(jnp.int32, (ROWS, 128), 1)
        key_total = value_total = None
        for block in range(blocks):
            own = pl.ds(pl.multiple_of(sequence * length + block * ROWS, ROWS), ROWS)
            same = fragment_column[sequence, block * ROWS : (block + 1) * ROWS, :] == fragment_row[sequence]
            q = queries[own, lanes].astype(jnp.float32) * (HEAD**-0.5)
            m = mixed_grad[own, lanes].astype(jnp.float32)
            totals = log_totals[own, :]
            results = []
            for h in range(2):
                part = (lane >= HEAD) if h else (lane < HEAD)
                qh = jnp.where(part, q, 0.0).astype(jnp.bfloat16)
                mh = jnp.where(part, m, 0.0).astype(jnp.bfloat16)
                level = jnp.sum(jnp.where(head_lane == 2 * pair + h, totals, 0.0), axis=-1, keepdims=True)
                weights = jnp.exp(jnp.where(same, cross(qh, k), -1000000000.0) - level)
                prob_grad = cross(mh, v)
                row = jnp.sum(prob_grad * weights, axis=-1, keepdims=True)
                score_grad = (weights * (prob_grad - row)).astype(jnp.bfloat16)
                results.append(jnp.dot(score_grad, k, preferred_element_type=jnp.float32) * (HEAD**-0.5))
                key_part = inward(score_grad, qh)
                value_part = inward(weights.astype(jnp.bfloat16), mh)
                key_total = key_part if key_total is None else key_total + key_part
                value_total = value_part if value_total is None else value_total + value_part
            query_grad[own, lanes] = jnp.where(lane < HEAD, results[0], results[1]).astype(jnp.bfloat16)
        key_grad[every, lanes] = key_total.astype(jnp.bfloat16)
        value_grad[every, lanes] = value_total.astype(jnp.bfloat16)
        return carry

    lax.fori_loop(0, steps, attend, 0)
    one[3]()
    for step in two[2]:
        step()
    one[4]()
    two[3]()
    two[4]()
    one[5]()
    two[5]()


def backward_all(
    grad_expand, grad_reduce, out_grad, out_weight, queries, key_rows, value_rows, log_totals, segment_ids
):
    low = jnp.bfloat16
    vmem, anywhere = pl.BlockSpec(memory_space=pltpu.VMEM), pl.BlockSpec(memory_space=pl.ANY)
    flat = jax.ShapeDtypeStruct(out_grad.shape, low)
    shapes = [grad_expand.shape[2:], grad_reduce.shape[2:]]
    return pl.pallas_call(
        backward_kernel,
        out_shape=[jax.ShapeDtypeStruct(s, low) for s in shapes] + [flat] * 3,
        in_specs=[anywhere, anywhere] + [vmem] * 8,
        out_specs=[vmem] * 5,
        scratch_shapes=[pltpu.VMEM(out_grad.shape, low)] + [x for s in shapes for x in scatter_scratch(*s)],
        compiler_params=pltpu.CompilerParams(
            collective_id=2, has_side_effects=True, vmem_limit_bytes=60 * 1024 * 1024
        ),
        name="backward",
    )(
        grad_expand, grad_reduce, out_grad, out_weight, queries, key_rows, value_rows, log_totals,
        segment_ids[:, :, None], segment_ids[:, None, :],
    )


def plain_on_device(
    tokens,
    segment_ids,
    query_weight,
    query_bias,
    key_weight,
    value_weight,
    value_bias,
    out_weight,
    out_bias,
    first_gain,
    first_shift,
    expand_weight,
    expand_bias,
    reduce_weight,
    reduce_bias,
    second_gain,
    second_shift,
    cotangent,
):
    seq_count, seq_length = segment_ids.shape
    shaped = (seq_count, seq_length, HEADS, HEAD)
    rows, width = query_weight.shape
    small = (query_bias, value_bias, out_bias, first_gain, first_shift, reduce_bias, second_gain, second_shift)
    small_pack = jnp.concatenate([v[None, :] for v in small] + [expand_bias.reshape(-1, rows)], axis=0)
    gathered_small = lax.all_gather(small_pack, "fsdp", axis=1, tiled=True)
    groups = gathered_small.shape[1] // rows
    vectors = [gathered_small[k] for k in range(8)]
    expand_bias_all = (
        gathered_small[8:].reshape(-1, groups, rows).transpose(1, 0, 2).reshape(groups * expand_bias.shape[0])
    )
    query_bias_all, value_bias_all, out_bias_all, gain1, shift1, reduce_bias_all, gain2, shift2 = vectors
    attention_pack = jnp.stack([query_weight, key_weight, value_weight, out_weight])
    attention_all = lax.all_gather(attention_pack, "fsdp", axis=1, tiled=True)
    expand_all = lax.all_gather(expand_weight, "fsdp", axis=0, tiled=True)
    reduce_all = lax.all_gather(reduce_weight, "fsdp", axis=0, tiled=True)
    wq, wk, wv, wo = attention_all[0], attention_all[1], attention_all[2], attention_all[3]

    queries = linear(tokens, wq, query_bias_all).astype(jnp.bfloat16).reshape(shaped)
    key_rows = jnp.dot(tokens, wk, preferred_element_type=jnp.float32).astype(jnp.bfloat16).reshape(shaped)
    value_rows = linear(tokens, wv, value_bias_all).astype(jnp.bfloat16).reshape(shaped)
    mixed, log_totals = lax.map(attend_forward, (queries, key_rows, value_rows, segment_ids))
    mixed = mixed.reshape(tokens.shape)
    first_sum = tokens.astype(jnp.float32) + linear(mixed, wo, out_bias_all)
    hidden, first_normed, first_rescale = layer_norm(first_sum, gain1, shift1)
    hidden_low = hidden.astype(jnp.bfloat16)
    inner = linear(hidden_low, expand_all, expand_bias_all)
    active = jax.nn.gelu(inner, approximate=False).astype(jnp.bfloat16)
    second_sum = hidden + linear(active, reduce_all, reduce_bias_all)
    output, second_normed, second_rescale = layer_norm(second_sum, gain2, shift2)
    second_grad, grad_second_gain, grad_second_shift = norm_back(
        cotangent.astype(jnp.float32), second_normed, second_rescale, gain2
    )
    branch_grad = second_grad.astype(jnp.bfloat16)
    grad_reduce = weight_grad(active, branch_grad)
    grad_reduce_bias = bias_grad(branch_grad)
    inner_grad = (back_rows(branch_grad, reduce_all) * gelu_slope(inner)).astype(jnp.bfloat16)
    grad_expand = weight_grad(hidden_low, inner_grad)
    grad_expand_bias = bias_grad(inner_grad)
    hidden_grad = second_grad + back_rows(inner_grad, expand_all)
    low = jnp.bfloat16
    scattered_expand = lax.psum_scatter(grad_expand.astype(low), "fsdp", scatter_dimension=0, tiled=True)
    scattered_reduce = lax.psum_scatter(grad_reduce.astype(low), "fsdp", scatter_dimension=0, tiled=True)
    first_grad, grad_first_gain, grad_first_shift = norm_back(
        hidden_grad, first_normed, first_rescale, gain1
    )
    out_grad = first_grad.astype(jnp.bfloat16)
    grad_out = weight_grad(mixed, out_grad)
    grad_out_bias = bias_grad(out_grad)
    mixed_grad = back_rows(out_grad, wo).astype(jnp.bfloat16).reshape(shaped)
    query_grad, key_grad, value_grad = lax.map(
        attend_backward, (queries, key_rows, value_rows, segment_ids, mixed_grad, log_totals)
    )
    query_grad = query_grad.reshape(tokens.shape)
    key_grad = key_grad.reshape(tokens.shape)
    value_grad = value_grad.reshape(tokens.shape)
    grad_query = weight_grad(tokens, query_grad)
    grad_query_bias = bias_grad(query_grad)
    grad_key = weight_grad(tokens, key_grad)
    grad_value = weight_grad(tokens, value_grad)
    grad_value_bias = bias_grad(value_grad)
    input_grad = first_grad + back_rows(query_grad, wq) + back_rows(key_grad, wk) + back_rows(value_grad, wv)
    small_grads = (
        grad_query_bias, grad_value_bias, grad_out_bias, grad_first_gain, grad_first_shift,
        grad_reduce_bias, grad_second_gain, grad_second_shift,
    )
    small_sum = jnp.concatenate(
        [v[None, :] for v in small_grads]
        + [grad_expand_bias.reshape(groups, -1, rows).transpose(1, 0, 2).reshape(-1, groups * rows)],
        axis=0,
    )
    small_sum = lax.psum(small_sum, ("dp", "fsdp"))
    at = lax.axis_index("fsdp") * rows
    small_own = lax.dynamic_slice_in_dim(small_sum, at, rows, axis=1)
    attention_grads = jnp.concatenate([grad_query, grad_key, grad_value, grad_out], axis=1).astype(low)
    attention_own = lax.psum_scatter(attention_grads, "fsdp", scatter_dimension=0, tiled=True)
    attention_own = lax.psum(attention_own, "dp").astype(jnp.float32)
    attention_own = [attention_own[:, k * width : (k + 1) * width] for k in range(4)]
    expand_own = lax.psum(scattered_expand, "dp").astype(jnp.float32)
    reduce_own = lax.psum(scattered_reduce, "dp").astype(jnp.float32)
    return (
        output.astype(jnp.bfloat16),
        input_grad,
        attention_own[0],
        small_own[0],
        attention_own[1],
        attention_own[2],
        small_own[1],
        attention_own[3],
        small_own[2],
        small_own[3],
        small_own[4],
        expand_own,
        small_own[8:].reshape(-1),
        reduce_own,
        small_own[5],
        small_own[6],
        small_own[7],
    )


def on_device(
    tokens,
    segment_ids,
    query_weight,
    query_bias,
    key_weight,
    value_weight,
    value_bias,
    out_weight,
    out_bias,
    first_gain,
    first_shift,
    expand_weight,
    expand_bias,
    reduce_weight,
    reduce_bias,
    second_gain,
    second_shift,
    cotangent,
):
    rows, width = query_weight.shape
    low = jnp.bfloat16
    me = lax.axis_index("fsdp")
    shards = 2 * LINE
    vectors = jnp.stack(
        [query_bias, value_bias, out_bias, first_gain, first_shift, reduce_bias, second_gain, second_shift]
    )
    count = expand_bias.shape[0]
    per_row = width // count
    small = lax.dynamic_update_slice(jnp.zeros((SMALL, width), low), vectors, (0, me * rows))
    small = lax.dynamic_update_slice(small, expand_bias[None, :], (8 + me // per_row, lax.rem(me, per_row) * count))
    pack = jnp.concatenate([query_weight, key_weight, value_weight, out_weight, small], axis=0)
    (
        attention_all, expand_all, reduce_all, queries, key_rows, value_rows, mixed, log_totals, first_normed, first_rescale,
    ) = forward_all(pack, expand_weight, reduce_weight, tokens, segment_ids)
    wq, wk, wv, wo = [attention_all[:, k * rows : (k + 1) * rows].reshape(width, width) for k in range(4)]
    small_all = jnp.sum(attention_all[:, 4 * rows :].astype(jnp.float32), axis=0)
    query_bias_all, value_bias_all, out_bias_all, gain1, shift1, reduce_bias_all, gain2, shift2 = [
        small_all[k] for k in range(8)
    ]
    expand_bias_all = small_all[8 : 8 + shards // per_row].reshape(-1)
    expand_all = expand_all.reshape(width, -1)
    reduce_all = reduce_all.reshape(-1, width)

    hidden = first_normed * gain1 + shift1
    hidden_low = hidden.astype(jnp.bfloat16)
    inner = linear(hidden_low, expand_all, expand_bias_all)
    active = jax.nn.gelu(inner, approximate=False).astype(jnp.bfloat16)
    second_sum = hidden + linear(active, reduce_all, reduce_bias_all)
    output, second_normed, second_rescale = layer_norm(second_sum, gain2, shift2)
    second_grad, grad_second_gain, grad_second_shift = norm_back(
        cotangent.astype(jnp.float32), second_normed, second_rescale, gain2
    )
    branch_grad = second_grad.astype(jnp.bfloat16)
    grad_reduce = weight_grad(active, branch_grad)
    grad_reduce_bias = bias_grad(branch_grad)
    inner_grad = (back_rows(branch_grad, reduce_all) * gelu_slope(inner)).astype(jnp.bfloat16)
    grad_expand = weight_grad(hidden_low, inner_grad)
    grad_expand_bias = bias_grad(inner_grad)
    hidden_grad = second_grad + back_rows(inner_grad, expand_all)
    first_grad, grad_first_gain, grad_first_shift = norm_back(
        hidden_grad, first_normed, first_rescale, gain1
    )
    out_grad = first_grad.astype(jnp.bfloat16)
    grad_out = weight_grad(mixed, out_grad)
    grad_out_bias = bias_grad(out_grad)
    expand_own, reduce_own, query_grad, key_grad, value_grad = backward_all(
        grad_expand.astype(low).reshape(LINE, 2, rows, -1),
        grad_reduce.astype(low).reshape(LINE, 2, -1, width),
        out_grad,
        wo,
        queries,
        key_rows,
        value_rows,
        log_totals,
        segment_ids,
    )
    grad_query = weight_grad(tokens, query_grad)
    grad_query_bias = bias_grad(query_grad)
    grad_key = weight_grad(tokens, key_grad)
    grad_value = weight_grad(tokens, value_grad)
    grad_value_bias = bias_grad(value_grad)
    input_grad = first_grad + back_rows(query_grad, wq) + back_rows(key_grad, wk) + back_rows(value_grad, wv)
    small_grads = (
        grad_query_bias, grad_value_bias, grad_out_bias, grad_first_gain, grad_first_shift,
        grad_reduce_bias, grad_second_gain, grad_second_shift,
    )
    small_grads = jnp.stack(small_grads).reshape(8, shards, rows).transpose(1, 0, 2)
    small_grads = jnp.concatenate([small_grads, grad_expand_bias.reshape(shards, -1, rows)], axis=1)
    small_grads = jnp.pad(
        small_grads.astype(low), ((0, 0), (0, SMALL - small_grads.shape[1]), (0, width - rows))
    )
    attention_grads = jnp.concatenate(
        [g.astype(low).reshape(shards, rows, width) for g in (grad_query, grad_key, grad_value, grad_out)]
        + [small_grads],
        axis=1,
    )
    (attention_own,) = scatter_all([attention_grads.reshape(LINE, 2, -1, width)], 3)
    attention_own = attention_own.astype(jnp.float32)
    small_own = attention_own[4 * rows :, :rows]
    attention_own = [attention_own[k * rows : (k + 1) * rows] for k in range(4)]
    return (
        output.astype(low),
        input_grad,
        attention_own[0],
        small_own[0],
        attention_own[1],
        attention_own[2],
        small_own[1],
        attention_own[3],
        small_own[2],
        small_own[3],
        small_own[4],
        expand_own.astype(jnp.float32),
        small_own[8 : 8 + count // rows].reshape(-1),
        reduce_own.astype(jnp.float32),
        small_own[5],
        small_own[6],
        small_own[7],
    )


def solution(mesh):
    fits = mesh.shape["fsdp"] == 2 * LINE and mesh.shape["dp"] == 4
    body = on_device if fits else plain_on_device
    in_specs = (
        P(("dp", "fsdp"), None),
        P(("dp", "fsdp"), None),
        P("fsdp", None),
        P("fsdp"),
        P("fsdp", None),
        P("fsdp", None),
        P("fsdp"),
        P("fsdp", None),
        P("fsdp"),
        P("fsdp"),
        P("fsdp"),
        P("fsdp", None),
        P("fsdp"),
        P("fsdp", None),
        P("fsdp"),
        P("fsdp"),
        P("fsdp"),
        P(("dp", "fsdp"), None),
    )
    out_specs = (
        P(("dp", "fsdp"), None),
        P(("dp", "fsdp"), None),
        P("fsdp", None),
        P("fsdp"),
        P("fsdp", None),
        P("fsdp", None),
        P("fsdp"),
        P("fsdp", None),
        P("fsdp"),
        P("fsdp"),
        P("fsdp"),
        P("fsdp", None),
        P("fsdp"),
        P("fsdp", None),
        P("fsdp"),
        P("fsdp"),
        P("fsdp"),
    )
    return jax.shard_map(
        body, mesh=mesh, in_specs=in_specs, out_specs=out_specs, check_vma=False
    )
```
